32 devices in a mesh: cfg: 2 (over x), sx: 16 (over z, y, core).
Axes of the slice: x: 2, y: 2, z: 4, core: 2. Of those that a mesh axis runs over, the one named last changes fastest.
Arguments:
- eigvecs: bfloat16 [512, 2, 3, 16, 1024], P('cfg', None, None, 'sx'), parts along dimension 0, may hold values from -6 to 6
- link_seed: int32 [6], P('cfg'), parts along dimension 0, may hold values from 1 to 46336
- ownership: int32 [2080], replicated, may hold values from 0 to 2079, each once
Outputs:
- elementals: float32 [4160, 96], P(('cfg', 'sx')), parts along dimension 0
The draws below stay inside these ranges and needn't reach their ends.
There are 2 independent parts, one for each index of `cfg`. The reference program is written for one: setup_inputs(seed, part) draws one part's arguments, and reference() takes and returns one part's arrays. A program takes and returns all parts, laid end to end along the dimension named above; an argument that names none is the same for every part. Nothing has to cross between parts.
Inputs may be any that keep to these rules, and one draw needn't show every extreme that they name: ownership is a permutation of the pair tiles 0 to 2079.
All inputs are finite; a program needn't handle non-finite values.
Results may differ from the reference program's by a relative error of at most 0.0029.
Values may be sent and summed in bfloat16 or wider, within the bound.
A program may use at most 192 MiB of HBM per device.

```python
import math
import jax
import jax.numpy as jnp
import numpy as np
from jax import lax

NEV = 256
TM = 4
NY = 16
NZ = 64
PLANE = 1024
NX = 16
PAIRS = 2080


def steps_of(stream_key, extent, pieces, low, high):
    gain = 1.0
    for axis_at, shards_of in pieces:
        steps = jax.random.uniform(jax.random.fold_in(jax.random.fold_in(stream_key, 6), axis_at), (shards_of,), jnp.float32, low / len(pieces), high / len(pieces))
        gain = gain * jnp.repeat(jnp.exp(steps), extent[axis_at] // shards_of).reshape((-1,) + (1,) * (len(extent) - 1 - axis_at))
    return gain


def scatter_about(rng, shape, scale, most, shards=(), kind=jnp.bfloat16):
    drawn = jax.random.normal(rng, shape, jnp.float32) * scale
    if len(shards) > 0:
        drawn = steps_of(rng, shape, shards, -0.22, 0.18) * drawn
    return jnp.clip(drawn, min=-most, max=most).astype(kind)


def setup_inputs(seed: int = 0, part: int = 0) -> dict:
    splits = jax.random.split(jax.random.key(seed), 4)
    part_splits = jax.random.split(jax.random.fold_in(splits[3], part), 4)
    return {
        "eigvecs": scatter_about(part_splits[0], (NEV, 2, 3, NX, PLANE), 1.0, 6.0, ((3, 16),)),
        "link_seed": jax.random.randint(part_splits[1], (3,), 1, 46337).astype(jnp.int32),
        "ownership": jax.random.permutation(splits[2], PAIRS).astype(jnp.int32),
    }


def scramble(seed_value, site_code):
    modulus = 46337
    low_part = site_code % modulus
    high_part = site_code // modulus
    mixed_value = (seed_value * seed_value + low_part) % modulus
    mixed_value = (mixed_value * mixed_value + high_part * 977 + 31) % modulus
    angles = []
    for angle_index in range(7):
        scrambled = (mixed_value + 5171 * angle_index + 1) % modulus
        scrambled = (scrambled * scrambled + low_part) % modulus
        scrambled = (scrambled * scrambled + 12345) % modulus
        angles.append(scrambled.astype(jnp.float32) * (2.0 * math.pi / modulus) - math.pi)
    return angles

def link_field(seed_value, site_code):
    angles = scramble(seed_value, site_code)
    cos_alpha, sin_alpha = (jnp.cos(angles[0]), jnp.sin(angles[0]))
    cos_beta, sin_beta = (jnp.cos(angles[1]), jnp.sin(angles[1]))
    cos_gamma, sin_gamma = (jnp.cos(angles[2]), jnp.sin(angles[2]))
    rotation = [[cos_alpha * cos_beta * cos_gamma - sin_alpha * sin_gamma, -cos_alpha * cos_beta * sin_gamma - sin_alpha * cos_gamma, cos_alpha * sin_beta], [sin_alpha * cos_beta * cos_gamma + cos_alpha * sin_gamma, -sin_alpha * cos_beta * sin_gamma + cos_alpha * cos_gamma, sin_alpha * sin_beta], [-sin_beta * cos_gamma, sin_beta * sin_gamma, cos_beta]]
    phase_left = [angles[3], angles[4], -angles[3] - angles[4]]
    phase_right = [angles[5], angles[6], -angles[5] - angles[6]]
    link_real = jnp.stack([jnp.stack([rotation[row_index][column] * jnp.cos(phase_left[row_index] + phase_right[column]) for column in range(3)]) for row_index in range(3)])
    link_imag = jnp.stack([jnp.stack([rotation[row_index][column] * jnp.sin(phase_left[row_index] + phase_right[column]) for column in range(3)]) for row_index in range(3)])
    return (link_real, link_imag)

def hop_vectors(link_real, link_imag, vectors):
    real_part = vectors[:, 0].astype(jnp.float32)
    imag_part = vectors[:, 1].astype(jnp.float32)
    out_real = []
    out_imag = []
    for colour in range(3):
        acc_real = jnp.zeros(real_part[:, 0].shape, jnp.float32)
        acc_imag = jnp.zeros(real_part[:, 0].shape, jnp.float32)
        for source in range(3):
            u_real = link_real[colour, source]
            u_imag = link_imag[colour, source]
            acc_real = acc_real + u_real * real_part[:, source] - u_imag * imag_part[:, source]
            acc_imag = acc_imag + u_real * imag_part[:, source] + u_imag * real_part[:, source]
        out_real.append(acc_real)
        out_imag.append(acc_imag)
    return jnp.stack([jnp.stack(out_real, 1), jnp.stack(out_imag, 1)], 1).astype(jnp.bfloat16)

def shift_plane(vectors, axis_number):
    shape = vectors.shape
    spread = vectors.reshape(shape[:4] + (NY, NZ))
    return jnp.roll(spread, -1, axis_number).reshape(shape)

def conjugate_stack(vectors):
    return jnp.concatenate([vectors, jnp.stack([-vectors[:, 1], vectors[:, 0]], 1)], 0)

def antisymmetric(products):
    real_part = products[:, 0] - jnp.swapaxes(products[:, 0], 1, 2)
    imag_part = products[:, 1] + jnp.swapaxes(products[:, 1], 1, 2)
    return jnp.stack([real_part, imag_part], 1)

def pick_tiles(products, chosen_rows):
    tile_count = NEV // TM
    tiles = products.reshape(3, 2, tile_count, TM, tile_count, TM).transpose(2, 4, 0, 1, 3, 5)
    return jnp.take(tiles.reshape(tile_count * tile_count, 6 * TM * TM), chosen_rows, axis=0)

def reference(eigvecs, link_seed, ownership):
    width = 6 * PLANE
    plane_index = jnp.arange(PLANE, dtype=jnp.int32)

    def layer_step(total, layer_index):
        layer = lax.dynamic_slice_in_dim(eigvecs, layer_index, 1, 3)
        upper_index = ((layer_index + 1) % NX).astype(jnp.int32)
        nearest = lax.dynamic_slice_in_dim(eigvecs, upper_index, 1, 3)
        site_code = (layer_index * PLANE + plane_index)[None, :]
        hop_x = hop_vectors(*link_field(link_seed[0], site_code), nearest)
        hop_y = hop_vectors(*link_field(link_seed[1], site_code), shift_plane(layer, 4))
        hop_z = hop_vectors(*link_field(link_seed[2], site_code), shift_plane(layer, 5))
        lefts = conjugate_stack(layer).reshape(2 * NEV, width).astype(jnp.float32)
        rights = jnp.concatenate([hop_x, hop_y, hop_z], 0).reshape(3 * NEV, width).astype(jnp.float32)
        term = lax.dot_general(lefts, rights, (((1,), (1,)), ((), ())), precision=lax.Precision.HIGHEST, preferred_element_type=jnp.float32)
        return (total + term, None)
    start_total = jnp.zeros((2 * NEV, 3 * NEV), jnp.float32)
    gram_matrix, _ = lax.scan(layer_step, start_total, jnp.arange(NX, dtype=jnp.int32))
    products = gram_matrix.reshape(2, NEV, 3, NEV).transpose(2, 0, 1, 3)
    normalise = 1.0 / math.sqrt(12.0 * NX * PLANE)
    derived = antisymmetric(products) * normalise
    upper_rows, upper_cols = np.triu_indices(NEV // TM)
    pair_rows = jnp.asarray((upper_rows * (NEV // TM) + upper_cols).astype(np.int32))
    chosen_rows = jnp.take(pair_rows, ownership)
    return pick_tiles(derived, chosen_rows)
```

```python
import functools
import math

import jax
import jax.numpy as jnp
from jax import lax
from jax.experimental import pallas as pl
from jax.experimental.pallas import tpu as pltpu
from jax.sharding import PartitionSpec as P

TM = 4
NZ = 64
MODULUS = 46337
LANES = 128
ROWS = 16
COLOURS = 3
LARGE = 48 * 1024 * 1024
MESH = pl.DeviceIdType.MESH
F32 = jnp.float32
BF16 = jnp.bfloat16
NT = (((1,), (1,)), ((), ()))


def quotient(value):
    q = jnp.floor(value.astype(F32) * (1.0 / MODULUS)).astype(jnp.int32)
    rest = value - q * MODULUS
    q = jnp.where(rest < 0, q - 1, jnp.where(rest >= MODULUS, q + 1, q))
    return q


def modulo(value):
    return value - quotient(value) * MODULUS


def links(seed, first_site, shape):
    code = (
        first_site
        + lax.broadcasted_iota(jnp.int32, shape, 0) * LANES
        + lax.broadcasted_iota(jnp.int32, shape, 1)
    )
    high = quotient(code)
    low = code - high * MODULUS
    mixed = modulo(seed * seed + low)
    mixed = modulo(mixed * mixed + high * 977 + 31)
    th = []
    for k in range(7):
        g = modulo(mixed + (5171 * k + 1))
        g = modulo(g * g + low)
        g = modulo(g * g + 12345)
        th.append(g.astype(F32) * (2.0 * math.pi / MODULUS) - math.pi)
    ca, sa = jnp.cos(th[0]), jnp.sin(th[0])
    cb, sb = jnp.cos(th[1]), jnp.sin(th[1])
    cg, sg = jnp.cos(th[2]), jnp.sin(th[2])
    rot = [
        [ca * cb * cg - sa * sg, -ca * cb * sg - sa * cg, ca * sb],
        [sa * cb * cg + ca * sg, -sa * cb * sg + ca * cg, sa * sb],
        [-sb * cg, sb * sg, cb],
    ]
    left = [th[3], th[4], -th[3] - th[4]]
    right = [th[5], th[6], -th[5] - th[6]]
    real, imag = [], []
    for r in range(3):
        for c in range(3):
            angle = left[r] + right[c]
            real.append(rot[r][c] * jnp.cos(angle))
            imag.append(rot[r][c] * jnp.sin(angle))
    return real + imag


def fill_hops(u_ref, d, src_ref, site, h_ref, slot):
    blocks, _, rows_all, _ = src_ref.shape
    after = lax.rem(site + 1, blocks)
    row = lax.broadcasted_iota(jnp.int32, (8, LANES), 0)
    lane = lax.broadcasted_iota(jnp.int32, (8, LANES), 1)
    even = row % 2 == 0
    sign = jnp.where(even, -1.0, 1.0).astype(F32)
    first_half = lane < NZ
    last = lane % NZ == NZ - 1

    def entry(e):
        return jnp.broadcast_to(u_ref[d, e, pl.ds(site, 1), :], (8, LANES))

    ur = [entry(e) for e in range(9)]
    ui = [entry(9 + e) * sign for e in range(9)]

    def rows_step(g, carry):
        rows = pl.ds(pl.multiple_of(g * ROWS, ROWS), ROWS)
        here = [src_ref[site, c, rows].astype(F32) for c in range(COLOURS)]
        if d == 1:
            there = [src_ref[after, c, rows].astype(F32) for c in range(COLOURS)]
        out = [[], [], []]
        for lo in (0, 8):
            v, s = [], []
            for c in range(COLOURS):
                x = here[c][lo : lo + 8]
                if d == 1:
                    x = jnp.where(first_half, there[c][lo : lo + 8], x)
                    x = pltpu.roll(x, LANES - NZ, 1)
                elif d == 2:
                    x = jnp.where(
                        last, pltpu.roll(x, NZ - 1, 1), pltpu.roll(x, LANES - 1, 1)
                    )
                v.append(x)
                s.append(jnp.where(even, pltpu.roll(x, 7, 0), pltpu.roll(x, 1, 0)))
            for c in range(COLOURS):
                total = None
                for k in range(COLOURS):
                    term = ur[3 * c + k] * v[k] + ui[3 * c + k] * s[k]
                    total = term if total is None else total + term
                out[c].append(total)
        for c in range(COLOURS):
            h_ref[slot, c, rows] = jnp.concatenate(out[c], 0).astype(BF16)
        return carry

    lax.fori_loop(0, rows_all // ROWS, rows_step, 0, unroll=2)


def add_products(v_ref, sites, h_ref, g_ref):
    left = jnp.concatenate(
        [v_ref[site, c] for site in sites for c in range(COLOURS)], 1
    )
    right = jnp.concatenate(
        [h_ref[slot, c] for slot in range(len(sites)) for c in range(COLOURS)], 1
    )
    g_ref[...] += lax.dot_general(left, right, NT, preferred_element_type=F32)


def derive(g_ref, c_ref, e_ref):
    both = g_ref.shape[0]
    modes = both // 2
    lane = lax.broadcasted_iota(jnp.int32, (modes, LANES), 1)
    even = lane % 2 == 0
    for n, j in enumerate(range(0, both, LANES)):
        for i in range(0, j + LANES, LANES):
            c_ref[n, i : i + LANES] = (
                g_ref[i : i + LANES, j : j + LANES]
                - g_ref[j : j + LANES, i : i + LANES].T
            )
        re_row = c_ref[n, pl.ds(0, modes, stride=2), :]
        im_row = c_ref[n, pl.ds(1, modes, stride=2), :]
        other = jnp.where(
            even, pltpu.roll(im_row, LANES - 1, 1), -pltpu.roll(im_row, 1, 1)
        )
        e_ref[:, j : j + LANES] = re_row + other


def prepare_slots(slot_ref, core, pad_ref, pick_ref, mask_ref, place_ref):
    devices, slots = slot_ref.shape
    rows = pad_ref.shape[1]
    modes = pick_ref.shape[2]
    tiles = modes // TM
    pad_ref[...] = jnp.full(pad_ref.shape, -1.0, F32)
    pad_ref[:, :slots] = slot_ref[...].astype(F32)
    columns = pad_ref[...].T
    mode = lax.broadcasted_iota(jnp.int32, (rows, modes), 1)
    i = mode // TM
    start = i * tiles - (i * (i - 1)) // 2
    lane = lax.broadcasted_iota(jnp.int32, (rows, 2 * modes), 1)
    for chip in range(devices // 2):
        pair = columns[:, 2 * chip : 2 * chip + 2]
        slot = jnp.where(core == 0, pair[:, :1], pair[:, 1:]).astype(jnp.int32)
        in_row = (slot >= start) & (slot < start + tiles - i)
        at = slice(chip * rows, (chip + 1) * rows)
        for r in range(TM):
            pick = jnp.where(in_row & (mode % TM == r), 1.0, 0.0)
            pick_ref[r, at] = pick.astype(BF16)
        i_of = jnp.max(jnp.where(in_row, i, 0), axis=1, keepdims=True)
        j_of = slot - (i_of * tiles - (i_of * (i_of - 1)) // 2) + i_of
        mask_ref[at] = jnp.where(lane // (2 * TM) == j_of, 1.0, 0.0)
    row = lax.broadcasted_iota(jnp.int32, (2 * modes, LANES), 0)
    col = lax.broadcasted_iota(jnp.int32, (2 * modes, LANES), 1)
    for d in range(3):
        for r in range(TM):
            target = ((2 * d + row % 2) * TM + r) * TM + (row // 2) % TM
            at = slice(r * 2 * modes, (r + 1) * 2 * modes)
            place_ref[d, at] = jnp.where(target == col, 1.0, 0.0).astype(BF16)


def main_kernel(
    scale,
    seed_ref,
    slot_ref,
    raw_ref,
    out_ref,
    own_ref,
    near_ref,
    u_ref,
    h_ref,
    g_ref,
    c_ref,
    e_ref,
    swap_ref,
    got_ref,
    sum_ref,
    pad_ref,
    pick_ref,
    mask_ref,
    place_ref,
    acc_ref,
    send_ref,
    came_ref,
    local_sems,
    plane_sems,
    swap_sems,
    piece_sems,
):
    cfg = lax.axis_index("cfg")
    me = lax.axis_index("sx")
    size = lax.axis_size("sx")
    chips = size // 2
    core = lax.rem(me, 2)
    chip = me // 2
    partner = (cfg, chip * 2 + 1 - core)
    below = (cfg, lax.rem(me + size - 1, size))
    modes, _, blocks, _, _ = raw_ref.shape
    rows = pad_ref.shape[1]
    slots, entries = out_ref.shape

    barrier = pltpu.get_barrier_semaphore()
    for step in range(1, size):
        pl.semaphore_signal(
            barrier,
            inc=1,
            device_id=(cfg, lax.rem(me + step, size)),
            device_id_type=MESH,
        )
    local = []
    for k in range(blocks):
        for c in range(COLOURS):
            local.append(
                pltpu.make_async_copy(
                    raw_ref.at[:, c, k], own_ref.at[k, c], local_sems.at[k, c]
                )
            )
            local[-1].start()
    first = me * (blocks * LANES)
    for d in (1, 2, 0):
        for e, value in enumerate(links(seed_ref[d], first, (blocks, LANES))):
            u_ref[d, e] = value
    pl.semaphore_wait(barrier, size - 1)
    planes = []
    for k in range(blocks):
        for c in range(COLOURS):
            local[k * COLOURS + c].wait()
        planes.append(
            pltpu.make_async_remote_copy(
                src_ref=own_ref.at[k],
                dst_ref=near_ref.at[k],
                send_sem=plane_sems.at[0, k],
                recv_sem=plane_sems.at[1, k],
                device_id=below,
                device_id_type=MESH,
            )
        )
        planes[-1].start()

    v = own_ref.reshape(blocks, COLOURS, 2 * modes, LANES)
    near = near_ref.reshape(blocks, COLOURS, 2 * modes, LANES)
    c_ref[...] = jnp.zeros_like(c_ref)
    swaps = {}

    def finish(d):
        derive(g_ref, c_ref, e_ref.at[d])
        swap_ref[d] = e_ref[d].astype(BF16)
        swaps[d] = pltpu.make_async_remote_copy(
            src_ref=swap_ref.at[d],
            dst_ref=got_ref.at[d],
            send_sem=swap_sems.at[0, d],
            recv_sem=swap_sems.at[1, d],
            device_id=partner,
            device_id_type=MESH,
        )
        swaps[d].start()

    def gather(d, at):
        found = []
        for r in range(TM):
            line = jnp.dot(
                pick_ref[r, at], sum_ref[...], preferred_element_type=F32
            )
            found.append((line * mask_ref[at]).astype(BF16))
        return jnp.dot(
            jnp.concatenate(found, 1), place_ref[d], preferred_element_type=F32
        )

    def piece_rows(to):
        return pl.ds(pl.multiple_of(to * rows, rows), rows)

    for d in (1, 2):
        g_ref[...] = jnp.zeros_like(g_ref)

        def pair_step(k, carry, d=d):
            sites = (2 * k, 2 * k + 1)
            for slot, site in enumerate(sites):
                fill_hops(u_ref, d, v, site, h_ref, slot)
            add_products(v, sites, h_ref, g_ref)
            return carry

        lax.fori_loop(0, blocks // 2, pair_step, 0)
        finish(d)

    prepare_slots(slot_ref, core, pad_ref, pick_ref, mask_ref, place_ref)
    for d in (1, 2):
        swaps[d].wait()
        sum_ref[...] = (e_ref[d] + got_ref[d].astype(F32)).astype(BF16)

        def spread_step(to, carry, d=d):
            at = piece_rows(to)
            found = gather(d, at)
            acc_ref[at] = found if d == 1 else acc_ref[at] + found
            return carry

        lax.fori_loop(0, chips, spread_step, 0)

    g_ref[...] = jnp.zeros_like(g_ref)

    def arrived(k):
        return pltpu.make_async_remote_copy(
            src_ref=own_ref.at[k],
            dst_ref=near_ref.at[k],
            send_sem=plane_sems.at[0, k],
            recv_sem=plane_sems.at[1, k],
            device_id=below,
            device_id_type=MESH,
        )

    def near_step(k, carry):
        sites = (2 * k, 2 * k + 1)
        for slot, site in enumerate(sites):
            arrived(site).wait_recv()
            fill_hops(u_ref, 0, near, site, h_ref, slot)
        add_products(v, sites, h_ref, g_ref)
        return carry

    lax.fori_loop(0, blocks // 2 - 1, near_step, 0)

    def last_step(k, carry):
        arrived(k).wait_recv()
        fill_hops(u_ref, 0, near, k, h_ref, 0)
        add_products(v, (k,), h_ref, g_ref)
        return carry

    lax.fori_loop(blocks - 2, blocks, last_step, 0)
    finish(0)
    swaps[0].wait()
    sum_ref[...] = (e_ref[0] + got_ref[0].astype(F32)).astype(BF16)

    def piece(step):
        to = lax.rem(chip + step, chips)
        return pltpu.make_async_remote_copy(
            src_ref=send_ref.at[to],
            dst_ref=came_ref.at[step],
            send_sem=piece_sems.at[0, step],
            recv_sem=piece_sems.at[1, step],
            device_id=(cfg, to * 2 + core),
            device_id_type=MESH,
        )

    def send_step(step, carry):
        to = lax.rem(chip + step, chips)
        at = piece_rows(to)
        send_ref[to] = (acc_ref[at] + gather(0, at)).astype(BF16)
        piece(step).start()
        return carry

    lax.fori_loop(1, chips, send_step, 0)
    at = piece_rows(chip)
    total = acc_ref[at] + gather(0, at)
    for step in range(1, chips):
        piece(step).wait_recv()
        total = total + came_ref[step].astype(F32)
    out_ref[...] = total[:slots, :entries] * scale
    for step in range(1, chips):
        piece(step).wait_send()
    for k in range(blocks):
        planes[k].wait_send()


def per_device(eigvecs, link_seed, ownership):
    modes, _, colours, layers, sites = eigvecs.shape
    size = lax.axis_size("sx")
    chips = size // 2
    blocks = sites // LANES
    raw = (
        eigvecs.transpose(0, 2, 3, 1, 4)
        .reshape(modes, colours, 2, blocks, LANES)
        .transpose(0, 1, 3, 2, 4)
    )
    slots = ownership.shape[0] // size
    rows = -(-slots // ROWS) * ROWS
    scale = 1.0 / math.sqrt(12.0 * layers * size * sites)
    vmem = pl.BlockSpec(memory_space=pltpu.VMEM)
    plane = pltpu.VMEM((blocks, colours, modes, 2, LANES), BF16)
    both = 2 * modes
    return pl.pallas_call(
        functools.partial(main_kernel, scale),
        out_shape=jax.ShapeDtypeStruct((slots, 6 * TM * TM), F32),
        in_specs=[
            pl.BlockSpec(memory_space=pltpu.SMEM),
            vmem,
            pl.BlockSpec(memory_space=pltpu.HBM),
        ],
        out_specs=vmem,
        scratch_shapes=[
            plane,
            plane,
            pltpu.VMEM((3, 18, blocks, LANES), F32),
            pltpu.VMEM((2, colours, both, LANES), BF16),
            pltpu.VMEM((both, both), F32),
            pltpu.VMEM((both // LANES, both, LANES), F32),
            pltpu.VMEM((3, modes, both), F32),
            pltpu.VMEM((3, modes, both), BF16),
            pltpu.VMEM((3, modes, both), BF16),
            pltpu.VMEM((modes, both), BF16),
            pltpu.VMEM((size, rows), F32),
            pltpu.VMEM((TM, chips * rows, modes), BF16),
            pltpu.VMEM((chips * rows, both), F32),
            pltpu.VMEM((3, TM * both, LANES), BF16),
            pltpu.VMEM((chips * rows, LANES), F32),
            pltpu.VMEM((chips, rows, LANES), BF16),
            pltpu.VMEM((chips, rows, LANES), BF16),
            pltpu.SemaphoreType.DMA((blocks, colours)),
            pltpu.SemaphoreType.DMA((2, blocks)),
            pltpu.SemaphoreType.DMA((2, 3)),
            pltpu.SemaphoreType.DMA((2, chips)),
        ],
        compiler_params=pltpu.CompilerParams(
            collective_id=0, has_side_effects=True, vmem_limit_bytes=LARGE
        ),
        name="elementals",
    )(link_seed, ownership.reshape(size, slots), raw)


def solution(mesh):
    return jax.shard_map(
        per_device,
        mesh=mesh,
        in_specs=(P("cfg", None, None, "sx", None), P("cfg"), P()),
        out_specs=P(("cfg", "sx"), None),
        check_vma=False,
    )
```

```python
import functools
import math

import jax
import jax.numpy as jnp
from jax import lax
from jax.experimental import pallas as pl
from jax.experimental.pallas import tpu as pltpu
from jax.sharding import PartitionSpec as P

TM = 4
NZ = 64
MODULUS = 46337
LANES = 128
ROWS = 16
COLOURS = 3
LARGE = 62 * 1024 * 1024
MESH = pl.DeviceIdType.MESH
F32 = jnp.float32
BF16 = jnp.bfloat16
NT = (((1,), (1,)), ((), ()))


def quotient(value):
    q = jnp.floor(value.astype(F32) * (1.0 / MODULUS)).astype(jnp.int32)
    rest = value - q * MODULUS
    q = jnp.where(rest < 0, q - 1, jnp.where(rest >= MODULUS, q + 1, q))
    return q


def modulo(value):
    return value - quotient(value) * MODULUS


def links(seed, code):
    high = quotient(code)
    low = code - high * MODULUS
    mixed = modulo(seed * seed + low)
    mixed = modulo(mixed * mixed + high * 977 + 31)
    th = []
    for k in range(7):
        g = modulo(mixed + (5171 * k + 1))
        g = modulo(g * g + low)
        g = modulo(g * g + 12345)
        th.append(g.astype(F32) * (2.0 * math.pi / MODULUS) - math.pi)
    ca, sa = jnp.cos(th[0]), jnp.sin(th[0])
    cb, sb = jnp.cos(th[1]), jnp.sin(th[1])
    cg, sg = jnp.cos(th[2]), jnp.sin(th[2])
    rot = [
        [ca * cb * cg - sa * sg, -ca * cb * sg - sa * cg, ca * sb],
        [sa * cb * cg + ca * sg, -sa * cb * sg + ca * cg, sa * sb],
        [-sb * cg, sb * sg, cb],
    ]
    left = [th[3], th[4], -th[3] - th[4]]
    right = [th[5], th[6], -th[5] - th[6]]
    real, imag = [], []
    for r in range(3):
        for c in range(3):
            angle = left[r] + right[c]
            real.append(rot[r][c] * jnp.cos(angle))
            imag.append(rot[r][c] * jnp.sin(angle))
    return real + imag


def behind(place, d, sites):
    if d == 1:
        return jnp.where(place < NZ, place + (sites - NZ), place - NZ)
    if d == 2:
        return jnp.where(place % NZ == 0, place + (NZ - 1), place - 1)
    return place


def shift_modes(v_ref, y_ref, z_ref):
    blocks = v_ref.shape[0]
    wide = 2 * LANES
    row = lax.broadcasted_iota(jnp.int32, (wide, LANES), 0)
    col = lax.broadcasted_iota(jnp.int32, (wide, LANES), 1)
    move_y = (row == col + (LANES - NZ)).astype(F32).astype(BF16)
    row = lax.broadcasted_iota(jnp.int32, (wide, wide), 0)
    col = lax.broadcasted_iota(jnp.int32, (wide, wide), 1)
    move_z = (row == behind(col, 2, wide)).astype(F32).astype(BF16)

    def step(k, carry):
        before = lax.rem(k + blocks - 1, blocks)
        for c in range(COLOURS):
            both = jnp.concatenate([v_ref[before, c], v_ref[k, c]], 1)
            moved = jnp.dot(both, move_y, preferred_element_type=F32)
            y_ref[k, c] = moved.astype(BF16)
        return carry

    def pair_step(k, carry):
        for c in range(COLOURS):
            both = jnp.concatenate([v_ref[2 * k, c], v_ref[2 * k + 1, c]], 1)
            moved = jnp.dot(both, move_z, preferred_element_type=F32).astype(BF16)
            z_ref[2 * k, c] = moved[:, :LANES]
            z_ref[2 * k + 1, c] = moved[:, LANES:]
        return carry

    lax.fori_loop(0, blocks, step, 0)
    lax.fori_loop(0, blocks // 2, pair_step, 0)


def widen(src_ref, site, f_ref):
    for c in range(COLOURS):
        f_ref[c] = src_ref[site, c].astype(F32)


def fill_hops(u_ref, d, f_ref, site, h_ref, slot):
    modes = f_ref.shape[1] // 2

    def entry(e):
        return jnp.broadcast_to(u_ref[d, e, pl.ds(site, 1), :], (8, LANES))

    u = [entry(e) for e in range(18)]

    def rows_step(g, carry):
        out = [[] for _ in range(6)]
        for lo in (0, 8):
            v = []
            for t in range(2):
                at = pl.multiple_of(2 * g * ROWS, 2 * ROWS) + 2 * lo + t
                for c in range(COLOURS):
                    v.append(f_ref[c, pl.ds(at, 8, stride=2), :])
            for c in range(COLOURS):
                re = im = None
                for k in range(COLOURS):
                    ur, ui = u[3 * c + k], u[9 + 3 * c + k]
                    p = ur * v[k] - ui * v[3 + k]
                    q = ur * v[3 + k] + ui * v[k]
                    re = p if re is None else re + p
                    im = q if im is None else im + q
                out[c].append(re)
                out[3 + c].append(im)
        for q in range(6):
            at = pl.multiple_of((q // 3) * modes + g * ROWS, ROWS)
            both = jnp.concatenate(out[q], 0).astype(BF16)
            h_ref[slot, q % 3, pl.ds(at, ROWS)] = both
        return carry

    lax.fori_loop(0, modes // ROWS, rows_step, 0, unroll=2)


def add_products(w_ref, sites, h_ref, g_ref):
    left = jnp.concatenate(
        [w_ref[site, c] for site in sites for c in range(COLOURS)], 1
    )
    right = jnp.concatenate(
        [h_ref[slot, c] for slot in range(len(sites)) for c in range(COLOURS)], 1
    )
    term = lax.dot_general(left, right, NT, preferred_element_type=F32)
    for n in range(g_ref.shape[0]):
        g_ref[n] += term[:, n * LANES : (n + 1) * LANES]


def derive(g_ref, s_ref, e_ref):
    parts, both, _ = g_ref.shape
    modes = both // 2
    count = parts // 2
    for n in range(count):
        here = [g_ref[n, pl.ds(t, modes, stride=2), :] for t in range(2)]
        there = [g_ref[count + n, pl.ds(t, modes, stride=2), :] for t in range(2)]
        s_ref[0, n] = here[0] + there[1]
        s_ref[1, n] = there[0] - here[1]
    for j in range(count):
        for i in range(j + 1):
            rows, cols = slice(i * LANES, (i + 1) * LANES), slice(j * LANES, (j + 1) * LANES)
            at = j * LANES
            e_ref[rows, at : at + LANES] = (
                s_ref[0, j, rows] - s_ref[0, i, cols].T
            ).astype(BF16)
            e_ref[rows, modes + at : modes + at + LANES] = (
                s_ref[1, j, rows] + s_ref[1, i, cols].T
            ).astype(BF16)


def prepare_slots(slot_ref, core, flat_ref, pick_ref, mask_ref, part_ref, place_ref):
    count = slot_ref.shape[1]
    chips, rows, modes = pick_ref.shape[0], pick_ref.shape[1] // TM, pick_ref.shape[2]
    tiles = modes // TM
    slots = count // (2 * chips)
    flat_ref[...] = jnp.full(flat_ref.shape, -1.0, F32)
    flat_ref[:, :count] = jnp.broadcast_to(slot_ref[...].astype(F32), (8, count))
    column = flat_ref[...].T[:, :1]
    mode = lax.broadcasted_iota(jnp.int32, (rows, modes), 1)
    i = mode // TM
    start = i * tiles - (i * (i - 1)) // 2
    lane = lax.broadcasted_iota(jnp.int32, (rows, LANES), 1)
    for chip in range(chips):
        at = 2 * chip * slots
        slot = jnp.where(
            core == 0, column[at : at + rows], column[at + slots : at + slots + rows]
        ).astype(jnp.int32)
        in_row = (slot >= start) & (slot < start + tiles - i)
        for r in range(TM):
            pick = jnp.where(in_row & (mode % TM == r), 1.0, 0.0)
            pick_ref[chip, r * rows : (r + 1) * rows] = pick.astype(BF16)
        i_of = jnp.max(jnp.where(in_row, i, 0), axis=1, keepdims=True)
        j_of = slot - (i_of * tiles - (i_of * (i_of - 1)) // 2) + i_of
        block = j_of // (LANES // TM)
        inside = j_of - block * (LANES // TM)
        part_ref[chip] = jnp.broadcast_to(block, (rows, LANES))
        mask_ref[chip] = jnp.where(lane // TM == inside, 1.0, 0.0)
    row = lax.broadcasted_iota(jnp.int32, (2 * TM * LANES, LANES), 0)
    col = lax.broadcasted_iota(jnp.int32, (2 * TM * LANES, LANES), 1)
    for d in range(3):
        r, t = row // (2 * LANES), (row // LANES) % 2
        target = ((2 * d + t) * TM + r) * TM + row % TM
        place_ref[d] = jnp.where(target == col, 1.0, 0.0).astype(BF16)


def main_kernel(
    scale,
    seed_ref,
    slot_ref,
    raw_ref,
    out_ref,
    own_ref,
    near_ref,
    y_ref,
    z_ref,
    u_ref,
    f_ref,
    h_ref,
    g_ref,
    s_ref,
    swap_ref,
    got_ref,
    sum_ref,
    flat_ref,
    pick_ref,
    mask_ref,
    part_ref,
    place_ref,
    acc_ref,
    send_ref,
    came_ref,
    slots_here,
    seeds_here,
    local_sems,
    small_sems,
    plane_sems,
    swap_sems,
    piece_sems,
):
    cfg = lax.axis_index("cfg")
    me = lax.axis_index("sx")
    size = lax.axis_size("sx")
    chips = size // 2
    core = lax.rem(me, 2)
    chip = me // 2
    partner = (cfg, chip * 2 + 1 - core)
    below = (cfg, lax.rem(me + size - 1, size))
    modes, _, blocks, _, _ = raw_ref.shape
    rows = send_ref.shape[1]
    slots, entries = out_ref.shape

    barrier = pltpu.get_barrier_semaphore()
    for step in range(1, size):
        pl.semaphore_signal(
            barrier,
            inc=1,
            device_id=(cfg, lax.rem(me + step, size)),
            device_id_type=MESH,
        )
    seed_copy = pltpu.make_async_copy(seed_ref, seeds_here, small_sems.at[0])
    seed_copy.start()
    local = []
    for k in range(blocks):
        for c in range(COLOURS):
            local.append(
                pltpu.make_async_copy(
                    raw_ref.at[:, c, k], own_ref.at[k, c], local_sems.at[k, c]
                )
            )
            local[-1].start()
    slot_copy = pltpu.make_async_copy(slot_ref, slots_here, small_sems.at[1])
    slot_copy.start()
    first = me * (blocks * LANES)
    position = lax.broadcasted_iota(
        jnp.int32, (blocks, LANES), 0
    ) * LANES + lax.broadcasted_iota(jnp.int32, (blocks, LANES), 1)
    seed_copy.wait()
    for d in (1, 2, 0):
        code = first + behind(position, d, blocks * LANES)
        for e, value in enumerate(links(seeds_here[d], code)):
            u_ref[d, e] = value
    pl.semaphore_wait(barrier, size - 1)

    def plane(k):
        return pltpu.make_async_remote_copy(
            src_ref=own_ref.at[k],
            dst_ref=near_ref.at[k],
            send_sem=plane_sems.at[0, k],
            recv_sem=plane_sems.at[1, k],
            device_id=below,
            device_id_type=MESH,
        )

    for k in range(blocks):
        for c in range(COLOURS):
            local[k * COLOURS + c].wait()
        plane(k).start()

    v = own_ref.reshape(blocks, COLOURS, 2 * modes, LANES)
    near = near_ref.reshape(blocks, COLOURS, 2 * modes, LANES)
    shift_modes(v, y_ref, z_ref)
    swap_ref[...] = jnp.zeros_like(swap_ref)
    g_ref[...] = jnp.zeros_like(g_ref)

    def swap(d):
        return pltpu.make_async_remote_copy(
            src_ref=swap_ref.at[d],
            dst_ref=got_ref.at[d],
            send_sem=swap_sems.at[0, d],
            recv_sem=swap_sems.at[1, d],
            device_id=partner,
            device_id_type=MESH,
        )

    def join(d):
        swap(d).wait()
        sum_ref[...] = (swap_ref[d].astype(F32) + got_ref[d].astype(F32)).astype(BF16)

    def gather(d, to):
        lines = jnp.dot(pick_ref[to], sum_ref[...], preferred_element_type=F32)
        part, mask = part_ref[to], mask_ref[to]
        found = []
        for r in range(TM):
            line = lines[r * rows : (r + 1) * rows]
            for t in range(2):
                at = t * modes
                x = line[:, at : at + LANES]
                for n in range(1, modes // LANES):
                    y = line[:, at + n * LANES : at + (n + 1) * LANES]
                    x = jnp.where(part == n, y, x)
                found.append((x * mask).astype(BF16))
        return jnp.dot(
            jnp.concatenate(found, 1), place_ref[d], preferred_element_type=F32
        )

    def pair_step(k, carry):
        sites = (2 * k, 2 * k + 1)
        for slot, site in enumerate(sites):
            widen(v, site, f_ref)
            fill_hops(u_ref, 1, f_ref, site, h_ref, slot)
            fill_hops(u_ref, 2, f_ref, site, h_ref, 2 + slot)
        add_products(y_ref, sites, h_ref.at[:2], g_ref.at[0])
        add_products(z_ref, sites, h_ref.at[2:], g_ref.at[1])
        return carry

    lax.fori_loop(0, blocks // 2, pair_step, 0)
    for d in (1, 2):
        derive(g_ref.at[d - 1], s_ref, swap_ref.at[d])
        swap(d).start()
    slot_copy.wait()
    prepare_slots(
        slots_here, core, flat_ref, pick_ref, mask_ref, part_ref, place_ref
    )
    for d in (1, 2):
        join(d)

        def spread_step(to, carry, d=d):
            found = gather(d, to)
            acc_ref[to] = found if d == 1 else acc_ref[to] + found
            return carry

        lax.fori_loop(0, chips, spread_step, 0)

    g_ref[0] = jnp.zeros(g_ref.shape[1:], F32)

    def near_step(k, carry):
        sites = (2 * k, 2 * k + 1)
        for slot, site in enumerate(sites):
            plane(site).wait_recv()
            widen(near, site, f_ref)
            fill_hops(u_ref, 0, f_ref, site, h_ref, slot)
        add_products(v, sites, h_ref, g_ref.at[0])
        return carry

    lax.fori_loop(0, blocks // 2 - 1, near_step, 0)

    def last_step(k, carry):
        plane(k).wait_recv()
        widen(near, k, f_ref)
        fill_hops(u_ref, 0, f_ref, k, h_ref, 0)
        add_products(v, (k,), h_ref, g_ref.at[0])
        return carry

    lax.fori_loop(blocks - 2, blocks, last_step, 0)
    derive(g_ref.at[0], s_ref, swap_ref.at[0])
    swap(0).start()
    join(0)

    def piece(step):
        to = lax.rem(chip + step, chips)
        return pltpu.make_async_remote_copy(
            src_ref=send_ref.at[to],
            dst_ref=came_ref.at[step],
            send_sem=piece_sems.at[0, step],
            recv_sem=piece_sems.at[1, step],
            device_id=(cfg, to * 2 + core),
            device_id_type=MESH,
        )

    def send_step(step, carry):
        to = lax.rem(chip + step, chips)
        send_ref[to] = (acc_ref[to] + gather(0, to)).astype(BF16)
        piece(step).start()
        return carry

    lax.fori_loop(1, chips, send_step, 0)
    total = acc_ref[chip] + gather(0, chip)
    for step in range(1, chips):
        piece(step).wait_recv()
        total = total + came_ref[step].astype(F32)
    out_ref[...] = total[:slots, :entries] * scale
    for step in range(1, chips):
        piece(step).wait_send()
    for k in range(blocks):
        plane(k).wait_send()


def per_device(eigvecs, link_seed, ownership):
    modes, _, colours, layers, sites = eigvecs.shape
    size = lax.axis_size("sx")
    chips = size // 2
    blocks = sites // LANES
    raw = (
        eigvecs.transpose(0, 2, 3, 1, 4)
        .reshape(modes, colours, 2, blocks, LANES)
        .transpose(0, 1, 3, 2, 4)
    )
    count = ownership.shape[0]
    slots = count // size
    rows = -(-slots // ROWS) * ROWS
    flat = -(-(count - slots + rows) // LANES) * LANES
    scale = 1.0 / math.sqrt(12.0 * layers * size * sites)
    vmem = pl.BlockSpec(memory_space=pltpu.VMEM)
    hbm = pl.BlockSpec(memory_space=pltpu.HBM)
    plane = pltpu.VMEM((blocks, colours, modes, 2, LANES), BF16)
    both = 2 * modes
    shifted = pltpu.VMEM((blocks, colours, both, LANES), BF16)
    derived = pltpu.VMEM((3, modes, both), BF16)
    return pl.pallas_call(
        functools.partial(main_kernel, scale),
        out_shape=jax.ShapeDtypeStruct((slots, 6 * TM * TM), F32),
        in_specs=[hbm, hbm, hbm],
        out_specs=vmem,
        scratch_shapes=[
            plane,
            plane,
            shifted,
            shifted,
            pltpu.VMEM((3, 18, blocks, LANES), F32),
            pltpu.VMEM((colours, both, LANES), F32),
            pltpu.VMEM((4, colours, both, LANES), BF16),
            pltpu.VMEM((2, both // LANES, both, LANES), F32),
            pltpu.VMEM((2, modes // LANES, modes, LANES), F32),
            derived,
            derived,
            pltpu.VMEM((modes, both), BF16),
            pltpu.VMEM((8, flat), F32),
            pltpu.VMEM((chips, TM * rows, modes), BF16),
            pltpu.VMEM((chips, rows, LANES), F32),
            pltpu.VMEM((chips, rows, LANES), jnp.int32),
            pltpu.VMEM((3, 2 * TM * LANES, LANES), BF16),
            pltpu.VMEM((chips, rows, LANES), F32),
            pltpu.VMEM((chips, rows, LANES), BF16),
            pltpu.VMEM((chips, rows, LANES), BF16),
            pltpu.VMEM((1, count), jnp.int32),
            pltpu.SMEM(link_seed.shape, jnp.int32),
            pltpu.SemaphoreType.DMA((blocks, colours)),
            pltpu.SemaphoreType.DMA((2,)),
            pltpu.SemaphoreType.DMA((2, blocks)),
            pltpu.SemaphoreType.DMA((2, 3)),
            pltpu.SemaphoreType.DMA((2, chips)),
        ],
        compiler_params=pltpu.CompilerParams(
            collective_id=0, has_side_effects=True, vmem_limit_bytes=LARGE
        ),
        name="elementals",
    )(link_seed, ownership.reshape(1, count), raw)


def solution(mesh):
    return jax.shard_map(
        per_device,
        mesh=mesh,
        in_specs=(P("cfg", None, None, "sx", None), P("cfg"), P()),
        out_specs=P(("cfg", "sx"), None),
        check_vma=False,
    )
```

```python
import functools
import math

import jax
import jax.numpy as jnp
from jax import lax
from jax.experimental import pallas as pl
from jax.experimental.pallas import tpu as pltpu
from jax.sharding import PartitionSpec as P

TM = 4
NZ = 64
MODULUS = 46337
LANES = 128
ROWS = 16
COLOURS = 3
GROUPS = 4
SUBLANES = 8
LARGE = 61 * 1024 * 1024
MESH = pl.DeviceIdType.MESH
F32 = jnp.float32
BF16 = jnp.bfloat16
NT = (((1,), (1,)), ((), ()))


def quotient(value):
    q = jnp.floor(value.astype(F32) * (1.0 / MODULUS)).astype(jnp.int32)
    rest = value - q * MODULUS
    q = jnp.where(rest < 0, q - 1, jnp.where(rest >= MODULUS, q + 1, q))
    return q


def modulo(value):
    return value - quotient(value) * MODULUS


def links(seed, code):
    high = quotient(code)
    low = code - high * MODULUS
    mixed = modulo(seed * seed + low)
    mixed = modulo(mixed * mixed + high * 977 + 31)
    th = []
    for k in range(7):
        g = modulo(mixed + (5171 * k + 1))
        g = modulo(g * g + low)
        g = modulo(g * g + 12345)
        th.append(g.astype(F32) * (2.0 * math.pi / MODULUS) - math.pi)
    ca, sa = jnp.cos(th[0]), jnp.sin(th[0])
    cb, sb = jnp.cos(th[1]), jnp.sin(th[1])
    cg, sg = jnp.cos(th[2]), jnp.sin(th[2])
    rot = [
        [ca * cb * cg - sa * sg, -ca * cb * sg - sa * cg, ca * sb],
        [sa * cb * cg + ca * sg, -sa * cb * sg + ca * cg, sa * sb],
        [-sb * cg, sb * sg, cb],
    ]
    left = [th[3], th[4], -th[3] - th[4]]
    right = [th[5], th[6], -th[5] - th[6]]
    real, imag = [], []
    for r in range(3):
        for c in range(3):
            angle = left[r] + right[c]
            real.append(rot[r][c] * jnp.cos(angle))
            imag.append(rot[r][c] * jnp.sin(angle))
    return real + imag


def behind(place, d, sites):
    if d == 1:
        return jnp.where(place < NZ, place + (sites - NZ), place - NZ)
    if d == 2:
        return jnp.where(place % NZ == 0, place + (NZ - 1), place - 1)
    return place


def shift_modes(v_ref, y_ref, z_ref):
    blocks = v_ref.shape[0]
    wide = 2 * LANES
    row = lax.broadcasted_iota(jnp.int32, (wide, wide), 0)
    col = lax.broadcasted_iota(jnp.int32, (wide, wide), 1)
    from_y = col + (LANES - NZ)
    from_z = LANES + behind(col - LANES, 2, wide)
    source = jnp.where(col < LANES, from_y, from_z)
    move = (row == source).astype(F32).astype(BF16)

    def step(k, carry):
        before = lax.rem(k + blocks - 1, blocks)
        for c in range(COLOURS):
            both = jnp.concatenate([v_ref[before, c], v_ref[k, c]], 1)
            moved = jnp.dot(both, move, preferred_element_type=F32).astype(BF16)
            y_ref[k, c] = moved[:, :LANES]
            z_ref[k, c] = moved[:, LANES:]
        return carry

    lax.fori_loop(0, blocks, step, 0)


def widen(src_ref, site, f_ref):
    for c in range(COLOURS):
        f_ref[c] = src_ref[site, c].astype(F32)


def fill_hops(u_ref, d, f_ref, site, h_ref, slot):
    modes = f_ref.shape[1] // 2

    def entry(e):
        return jnp.broadcast_to(u_ref[d, e, pl.ds(site, 1), :], (8, LANES))

    u = [entry(e) for e in range(18)]

    def rows_step(g, carry):
        out = [[] for _ in range(6)]
        for lo in (0, 8):
            v = []
            for t in range(2):
                at = pl.multiple_of(2 * g * ROWS, 2 * ROWS) + 2 * lo + t
                for c in range(COLOURS):
                    v.append(f_ref[c, pl.ds(at, 8, stride=2), :])
            for c in range(COLOURS):
                re = im = None
                for k in range(COLOURS):
                    ur, ui = u[3 * c + k], u[9 + 3 * c + k]
                    p = ur * v[k] - ui * v[3 + k]
                    q = ur * v[3 + k] + ui * v[k]
                    re = p if re is None else re + p
                    im = q if im is None else im + q
                out[c].append(re)
                out[3 + c].append(im)
        for q in range(6):
            at = pl.multiple_of((q // 3) * modes + g * ROWS, ROWS)
            both = jnp.concatenate(out[q], 0).astype(BF16)
            h_ref[slot, q % 3, pl.ds(at, ROWS)] = both
        return carry

    lax.fori_loop(0, modes // ROWS, rows_step, 0, unroll=2)


def add_products(w_ref, sites, h_ref, g_ref):
    left = jnp.concatenate(
        [w_ref[site, c] for site in sites for c in range(COLOURS)], 1
    )
    right = jnp.concatenate(
        [h_ref[slot, c] for slot in range(len(sites)) for c in range(COLOURS)], 1
    )
    term = lax.dot_general(left, right, NT, preferred_element_type=F32)
    for n in range(g_ref.shape[0]):
        g_ref[n] += term[:, n * LANES : (n + 1) * LANES]


def derive(g_ref, s_ref, e_ref):
    parts, both, _ = g_ref.shape
    modes = both // 2
    count = parts // 2
    for n in range(count):
        here = [g_ref[n, pl.ds(t, modes, stride=2), :] for t in range(2)]
        there = [g_ref[count + n, pl.ds(t, modes, stride=2), :] for t in range(2)]
        s_ref[0, n] = here[0] + there[1]
        s_ref[1, n] = there[0] - here[1]
    for j in range(count):
        for i in range(j + 1):
            rows, cols = slice(i * LANES, (i + 1) * LANES), slice(j * LANES, (j + 1) * LANES)
            at = j * LANES
            e_ref[rows, at : at + LANES] = (
                s_ref[0, j, rows] - s_ref[0, i, cols].T
            ).astype(BF16)
            e_ref[rows, modes + at : modes + at + LANES] = (
                s_ref[1, j, rows] + s_ref[1, i, cols].T
            ).astype(BF16)


def prepare_slots(slot_ref, core, flat_ref, pick_ref, mask_ref, part_ref, place_ref):
    count = slot_ref.shape[0]
    chips, rows, modes = pick_ref.shape[0], pick_ref.shape[1] // TM, pick_ref.shape[2]
    tiles = modes // TM
    slots = count // (2 * chips)
    slot = slot_ref[...].reshape(1, count)

    def start(i):
        return i * tiles - (i * (i - 1)) // 2

    edge = 2 * tiles + 1
    root = jnp.sqrt((edge * edge - 8 * slot).astype(F32))
    i = jnp.floor((edge - root) * 0.5).astype(jnp.int32)
    i = jnp.where(start(i) > slot, i - 1, jnp.where(start(i + 1) <= slot, i + 1, i))
    j = slot - start(i) + i
    flat_ref[...] = jnp.full(flat_ref.shape, -1.0, F32)
    flat_ref[0:1, :count] = i.astype(F32)
    flat_ref[1:2, :count] = j.astype(F32)
    column = flat_ref[...].T
    mode = lax.broadcasted_iota(jnp.int32, (rows, modes), 1)
    lane = lax.broadcasted_iota(jnp.int32, (rows, LANES), 1)
    for chip in range(chips):
        at = 2 * chip * slots
        parts = []
        for g in range(GROUPS):
            lo = at + g * (-(-slots // GROUPS))
            part = jnp.where(
                core == 0,
                column[lo : lo + rows // GROUPS, :2],
                column[lo + slots : lo + slots + rows // GROUPS, :2],
            )
            parts.append(part)
        both = jnp.concatenate(parts, 0).astype(jnp.int32)
        i_of, j_of = both[:, :1] * TM, both[:, 1:]
        for r in range(TM):
            pick = jnp.where(mode == i_of + r, 1.0, 0.0)
            pick_ref[chip, r * rows : (r + 1) * rows] = pick.astype(BF16)
        block = j_of // (LANES // TM)
        inside = j_of - block * (LANES // TM)
        part_ref[chip] = jnp.broadcast_to(block, (rows, LANES))
        mask_ref[chip] = jnp.where(lane // TM == inside, 1.0, 0.0)
    row = lax.broadcasted_iota(jnp.int32, (2 * TM * LANES, LANES), 0)
    col = lax.broadcasted_iota(jnp.int32, (2 * TM * LANES, LANES), 1)
    r, t = row // (2 * LANES), (row // LANES) % 2
    target = (t * TM + r) * TM + row % TM
    width = 2 * TM * TM
    for n in range(place_ref.shape[0]):
        place_ref[n] = jnp.where(target + n * width == col, 1.0, 0.0).astype(BF16)


def main_kernel(
    scale,
    seed_ref,
    slot_ref,
    raw_ref,
    out_ref,
    own_ref,
    near_ref,
    y_ref,
    z_ref,
    u_ref,
    f_ref,
    h_ref,
    g_ref,
    s_ref,
    swap_ref,
    got_ref,
    sum_ref,
    flat_ref,
    pick_ref,
    mask_ref,
    part_ref,
    place_ref,
    acc_ref,
    send_ref,
    came_ref,
    send_yz_ref,
    came_yz_ref,
    slots_here,
    seeds_here,
    local_sems,
    small_sems,
    plane_sems,
    swap_sems,
    piece_sems,
):
    cfg = lax.axis_index("cfg")
    me = lax.axis_index("sx")
    size = lax.axis_size("sx")
    chips = size // 2
    core = lax.rem(me, 2)
    chip = me // 2
    partner = (cfg, chip * 2 + 1 - core)
    below = (cfg, lax.rem(me + size - 1, size))
    modes, _, blocks, _, _ = raw_ref.shape
    rows = mask_ref.shape[1]
    slots = out_ref.shape[0]

    barrier = pltpu.get_barrier_semaphore()
    for step in range(1, size):
        pl.semaphore_signal(
            barrier,
            inc=1,
            device_id=(cfg, lax.rem(me + step, size)),
            device_id_type=MESH,
        )
    seed_copy = pltpu.make_async_copy(seed_ref, seeds_here, small_sems.at[0])
    seed_copy.start()
    local = []
    for k in range(blocks):
        for c in range(COLOURS):
            local.append(
                pltpu.make_async_copy(
                    raw_ref.at[:, c, k], own_ref.at[k, c], local_sems.at[k, c]
                )
            )
            local[-1].start()
    slot_copy = pltpu.make_async_copy(slot_ref, slots_here, small_sems.at[1])
    slot_copy.start()
    first = me * (blocks * LANES)
    position = lax.broadcasted_iota(
        jnp.int32, (blocks, LANES), 0
    ) * LANES + lax.broadcasted_iota(jnp.int32, (blocks, LANES), 1)
    seed_copy.wait()
    for d in (1, 2, 0):
        code = first + behind(position, d, blocks * LANES)
        for e, value in enumerate(links(seeds_here[d], code)):
            u_ref[d, e] = value
    pl.semaphore_wait(barrier, size - 1)

    def plane(k):
        return pltpu.make_async_remote_copy(
            src_ref=own_ref.at[k],
            dst_ref=near_ref.at[k],
            send_sem=plane_sems.at[0, k],
            recv_sem=plane_sems.at[1, k],
            device_id=below,
            device_id_type=MESH,
        )

    for k in range(blocks):
        for c in range(COLOURS):
            local[k * COLOURS + c].wait()
        plane(k).start()

    v = own_ref.reshape(blocks, COLOURS, 2 * modes, LANES)
    near = near_ref.reshape(blocks, COLOURS, 2 * modes, LANES)
    shift_modes(v, y_ref, z_ref)
    swap_ref[...] = jnp.zeros_like(swap_ref)
    g_ref[...] = jnp.zeros_like(g_ref)

    def swap(d):
        return pltpu.make_async_remote_copy(
            src_ref=swap_ref.at[d],
            dst_ref=got_ref.at[d],
            send_sem=swap_sems.at[0, d],
            recv_sem=swap_sems.at[1, d],
            device_id=partner,
            device_id_type=MESH,
        )

    def join(d):
        swap(d).wait()
        sum_ref[d] = (swap_ref[d].astype(F32) + got_ref[d].astype(F32)).astype(BF16)

    def pick(d, to):
        part, mask = part_ref[to], mask_ref[to]
        lines = jnp.dot(pick_ref[to], sum_ref[d], preferred_element_type=F32)
        found = []
        for r in range(TM):
            line = lines[r * rows : (r + 1) * rows]
            for t in range(2):
                at = t * modes
                x = line[:, at : at + LANES]
                for n in range(1, modes // LANES):
                    y = line[:, at + n * LANES : at + (n + 1) * LANES]
                    x = jnp.where(part == n, y, x)
                found.append((x * mask).astype(BF16))
        return jnp.concatenate(found, 1)

    def gather(ds, to):
        found = jnp.concatenate([pick(d, to) for d in ds], 1)
        place = jnp.concatenate([place_ref[m] for m in range(len(ds))], 0)
        lines = jnp.dot(found, place, preferred_element_type=F32)
        sets = GROUPS // len(ds)
        each = rows // sets
        total = lines[:each]
        for n in range(1, sets):
            line = lines[n * each : (n + 1) * each]
            total = total + pltpu.roll(line, n * (LANES // sets), 1)
        return total

    def target(n):
        upper = (2 * chip) // chips
        rising = n + (n - chip + chips) // chips
        falling = chips - 1 - n
        falling = falling - (chip - falling + chips) // chips
        return upper * rising + (1 - upper) * falling

    def piece(kind, to, origin):
        send, came = ((send_ref, came_ref), (send_yz_ref, came_yz_ref))[kind]
        return pltpu.make_async_remote_copy(
            src_ref=send.at[to],
            dst_ref=came.at[origin],
            send_sem=piece_sems.at[2 * kind, to],
            recv_sem=piece_sems.at[2 * kind + 1, origin],
            device_id=(cfg, to * 2 + core),
            device_id_type=MESH,
        )

    def post(kind, ds):
        send = (send_ref, send_yz_ref)[kind]

        def post_step(n, carry):
            to = target(n)
            send[to] = gather(ds, to).astype(BF16)
            if kind == 0:
                piece(kind, to, chip).start()
            return carry

        lax.fori_loop(0, chips - 1, post_step, 0)
        return gather(ds, chip)

    def collect(kind, total):
        came = (came_ref, came_yz_ref)[kind]
        for step in range(1, chips):
            origin = lax.rem(chip + step, chips)
            piece(kind, origin, origin).wait_recv()
            total = total + came[origin].astype(F32)
        return total * scale

    def sent(kind):
        for step in range(1, chips):
            piece(kind, lax.rem(chip + step, chips), chip).wait_send()

    def pair_step(k, carry):
        sites = (2 * k, 2 * k + 1)
        for slot, site in enumerate(sites):
            widen(v, site, f_ref)
            fill_hops(u_ref, 1, f_ref, site, h_ref, slot)
            fill_hops(u_ref, 2, f_ref, site, h_ref, 2 + slot)
        add_products(y_ref, sites, h_ref.at[:2], g_ref.at[0])
        add_products(z_ref, sites, h_ref.at[2:], g_ref.at[1])
        return carry

    lax.fori_loop(0, blocks // 2, pair_step, 0)
    for d in (1, 2):
        derive(g_ref.at[d - 1], s_ref, swap_ref.at[d])
        swap(d).start()
    slot_copy.wait()
    prepare_slots(
        slots_here, core, flat_ref, pick_ref, mask_ref, part_ref, place_ref
    )
    for d in (1, 2):
        join(d)

    acc_ref[...] = post(1, (1, 2))
    g_ref[0] = jnp.zeros(g_ref.shape[1:], F32)

    def near_step(k, carry):
        sites = (2 * k, 2 * k + 1)
        for slot, site in enumerate(sites):
            plane(site).wait_recv()
            widen(near, site, f_ref)
            fill_hops(u_ref, 0, f_ref, site, h_ref, slot)
        add_products(v, sites, h_ref, g_ref.at[0])
        return carry

    lax.fori_loop(0, blocks // 2 - 1, near_step, 0)

    def use_plane(k):
        widen(near, k, f_ref)
        fill_hops(u_ref, 0, f_ref, k, h_ref, 0)
        add_products(v, (k,), h_ref, g_ref.at[0])

    plane(blocks - 2).wait_recv()
    use_plane(blocks - 2)
    plane(blocks - 1).wait_send()
    plane(blocks - 1).wait_recv()

    def launch_step(n, carry):
        piece(1, target(n), chip).start()
        return carry

    lax.fori_loop(0, chips - 1, launch_step, 0)
    use_plane(blocks - 1)
    derive(g_ref.at[0], s_ref, swap_ref.at[0])
    swap(0).start()
    join(0)

    here = post(0, (0,))
    acc_ref[...] = collect(1, acc_ref[...])
    total = collect(0, here)
    per = -(-slots // GROUPS)
    each = rows // GROUPS
    width = 2 * TM * TM
    for g in range(GROUPS):
        take = min(per, slots - g * per)
        first_rows = slice((g % 2) * each, (g % 2) * each + take)
        lanes = slice((g // 2) * 2 * width, (g // 2 + 1) * 2 * width)
        at = slice(g * per, g * per + take)
        out_ref[at, :width] = total[:take, g * width : (g + 1) * width]
        out_ref[at, width:] = acc_ref[first_rows, lanes]
    sent(0)
    sent(1)
    for k in range(blocks - 1):
        plane(k).wait_send()


def per_device(eigvecs, link_seed, ownership):
    modes, _, colours, layers, sites = eigvecs.shape
    size = lax.axis_size("sx")
    chips = size // 2
    blocks = sites // LANES
    raw = (
        eigvecs.transpose(0, 2, 3, 1, 4)
        .reshape(modes, colours, 2, blocks, LANES)
        .transpose(0, 1, 3, 2, 4)
    )
    count = ownership.shape[0]
    slots = count // size
    per = -(-slots // GROUPS)
    each = -(-per // SUBLANES) * SUBLANES
    rows = GROUPS * each
    flat = -(-(count - slots + (GROUPS - 1) * per + each) // LANES) * LANES
    scale = 1.0 / math.sqrt(12.0 * layers * size * sites)
    vmem = pl.BlockSpec(memory_space=pltpu.VMEM)
    hbm = pl.BlockSpec(memory_space=pltpu.HBM)
    plane = pltpu.VMEM((blocks, colours, modes, 2, LANES), BF16)
    both = 2 * modes
    shifted = pltpu.VMEM((blocks, colours, both, LANES), BF16)
    derived = pltpu.VMEM((3, modes, both), BF16)
    return pl.pallas_call(
        functools.partial(main_kernel, scale),
        out_shape=jax.ShapeDtypeStruct((slots, 6 * TM * TM), F32),
        in_specs=[hbm, hbm, hbm],
        out_specs=vmem,
        scratch_shapes=[
            plane,
            plane,
            shifted,
            shifted,
            pltpu.VMEM((3, 18, blocks, LANES), F32),
            pltpu.VMEM((colours, both, LANES), F32),
            pltpu.VMEM((4, colours, both, LANES), BF16),
            pltpu.VMEM((2, both // LANES, both, LANES), F32),
            pltpu.VMEM((2, modes // LANES, modes, LANES), F32),
            derived,
            derived,
            derived,
            pltpu.VMEM((8, flat), F32),
            pltpu.VMEM((chips, TM * rows, modes), BF16),
            pltpu.VMEM((chips, rows, LANES), F32),
            pltpu.VMEM((chips, rows, LANES), jnp.int32),
            pltpu.VMEM((2, 2 * TM * LANES, LANES), BF16),
            pltpu.VMEM((2 * each, LANES), F32),
            pltpu.VMEM((chips, each, LANES), BF16),
            pltpu.VMEM((chips, each, LANES), BF16),
            pltpu.VMEM((chips, 2 * each, LANES), BF16),
            pltpu.VMEM((chips, 2 * each, LANES), BF16),
            pltpu.VMEM((count,), jnp.int32),
            pltpu.SMEM(link_seed.shape, jnp.int32),
            pltpu.SemaphoreType.DMA((blocks, colours)),
            pltpu.SemaphoreType.DMA((2,)),
            pltpu.SemaphoreType.DMA((2, blocks)),
            pltpu.SemaphoreType.DMA((2, 3)),
            pltpu.SemaphoreType.DMA((4, chips)),
        ],
        compiler_params=pltpu.CompilerParams(
            collective_id=0, has_side_effects=True, vmem_limit_bytes=LARGE
        ),
        name="elementals",
    )(link_seed, ownership, raw)


def solution(mesh):
    return jax.shard_map(
        per_device,
        mesh=mesh,
        in_specs=(P("cfg", None, None, "sx", None), P("cfg"), P()),
        out_specs=P(("cfg", "sx"), None),
        check_vma=False,
    )
```

```python
import functools
import math

import jax
import jax.numpy as jnp
from jax import lax
from jax.experimental import pallas as pl
from jax.experimental.pallas import tpu as pltpu
from jax.sharding import PartitionSpec as P

TM = 4
NZ = 64
MODULUS = 46337
LANES = 128
ROWS = 16
COLOURS = 3
GROUPS = 4
SUBLANES = 8
LARGE = 52 * 1024 * 1024
MESH = pl.DeviceIdType.MESH
F32 = jnp.float32
BF16 = jnp.bfloat16
NT = (((1,), (1,)), ((), ()))


def quotient(value):
    q = jnp.floor(value.astype(F32) * (1.0 / MODULUS)).astype(jnp.int32)
    rest = value - q * MODULUS
    q = jnp.where(rest < 0, q - 1, jnp.where(rest >= MODULUS, q + 1, q))
    return q


def modulo(value):
    return value - quotient(value) * MODULUS


def links(seed, code):
    high = quotient(code)
    low = code - high * MODULUS
    mixed = modulo(seed * seed + low)
    mixed = modulo(mixed * mixed + high * 977 + 31)
    th = []
    for k in range(7):
        g = modulo(mixed + (5171 * k + 1))
        g = modulo(g * g + low)
        g = modulo(g * g + 12345)
        th.append(g.astype(F32) * (2.0 * math.pi / MODULUS) - math.pi)
    ca, sa = jnp.cos(th[0]), jnp.sin(th[0])
    cb, sb = jnp.cos(th[1]), jnp.sin(th[1])
    cg, sg = jnp.cos(th[2]), jnp.sin(th[2])
    rot = [
        [ca * cb * cg - sa * sg, -ca * cb * sg - sa * cg, ca * sb],
        [sa * cb * cg + ca * sg, -sa * cb * sg + ca * cg, sa * sb],
        [-sb * cg, sb * sg, cb],
    ]
    left = [th[3], th[4], -th[3] - th[4]]
    right = [th[5], th[6], -th[5] - th[6]]
    real, imag = [], []
    for r in range(3):
        for c in range(3):
            angle = left[r] + right[c]
            real.append(rot[r][c] * jnp.cos(angle))
            imag.append(rot[r][c] * jnp.sin(angle))
    return real + imag


def behind(place, d, sites):
    if d == 1:
        return jnp.where(place < NZ, place + (sites - NZ), place - NZ)
    if d == 2:
        return jnp.where(place % NZ == 0, place + (NZ - 1), place - 1)
    return place


def shift_modes(v_ref, y_ref, z_ref):
    blocks = v_ref.shape[0]
    wide = 2 * LANES
    row = lax.broadcasted_iota(jnp.int32, (wide, wide), 0)
    col = lax.broadcasted_iota(jnp.int32, (wide, wide), 1)
    from_y = col + (LANES - NZ)
    from_z = LANES + behind(col - LANES, 2, wide)
    source = jnp.where(col < LANES, from_y, from_z)
    move = (row == source).astype(F32).astype(BF16)

    def step(k, carry):
        before = lax.rem(k + blocks - 1, blocks)
        for c in range(COLOURS):
            both = jnp.concatenate([v_ref[before, c], v_ref[k, c]], 1)
            moved = jnp.dot(both, move, preferred_element_type=F32).astype(BF16)
            y_ref[k, c] = moved[:, :LANES]
            z_ref[k, c] = moved[:, LANES:]
        return carry

    lax.fori_loop(0, blocks, step, 0)


def widen(src_ref, site, f_ref, lo=0, hi=None):
    rows = slice(2 * lo, f_ref.shape[1] if hi is None else 2 * hi)
    for c in range(COLOURS):
        f_ref[c, rows] = src_ref[site, c, rows].astype(F32)


def fill_hops(u_ref, d, f_ref, site, h_ref, slot, lo=0, hi=None):
    modes = f_ref.shape[1] // 2
    hi = modes if hi is None else hi

    def entry(e):
        return jnp.broadcast_to(u_ref[d, e, pl.ds(site, 1), :], (8, LANES))

    u = [entry(e) for e in range(18)]

    def rows_step(g, carry):
        out = [[] for _ in range(6)]
        for lo in (0, 8):
            v = []
            for t in range(2):
                at = pl.multiple_of(2 * g * ROWS, 2 * ROWS) + 2 * lo + t
                for c in range(COLOURS):
                    v.append(f_ref[c, pl.ds(at, 8, stride=2), :])
            for c in range(COLOURS):
                re = im = None
                for k in range(COLOURS):
                    ur, ui = u[3 * c + k], u[9 + 3 * c + k]
                    p = ur * v[k] - ui * v[3 + k]
                    q = ur * v[3 + k] + ui * v[k]
                    re = p if re is None else re + p
                    im = q if im is None else im + q
                out[c].append(re)
                out[3 + c].append(im)
        for q in range(6):
            at = pl.multiple_of((q // 3) * modes + g * ROWS, ROWS)
            both = jnp.concatenate(out[q], 0).astype(BF16)
            h_ref[slot, q % 3, pl.ds(at, ROWS)] = both
        return carry

    lax.fori_loop(lo // ROWS, hi // ROWS, rows_step, 0, unroll=2)


def add_products(w_ref, sites, h_ref, g_ref):
    left = jnp.concatenate(
        [w_ref[site, c] for site in sites for c in range(COLOURS)], 1
    )
    right = jnp.concatenate(
        [h_ref[slot, c] for slot in range(len(sites)) for c in range(COLOURS)], 1
    )
    term = lax.dot_general(left, right, NT, preferred_element_type=F32)
    for n in range(g_ref.shape[0]):
        g_ref[n] += term[:, n * LANES : (n + 1) * LANES]


def add_block(w_ref, site, h_ref, g_ref, n):
    modes = h_ref.shape[2] // 2
    left = jnp.concatenate([w_ref[site, c] for c in range(COLOURS)], 1)
    rows = [slice(t * modes + n * LANES, t * modes + (n + 1) * LANES) for t in range(2)]
    right = jnp.concatenate(
        [
            jnp.concatenate([h_ref[0, c, at] for c in range(COLOURS)], 1)
            for at in rows
        ],
        0,
    )
    term = lax.dot_general(left, right, NT, preferred_element_type=F32)
    g_ref[n] += term[:, :LANES]
    g_ref[modes // LANES + n] += term[:, LANES:]


def derive(g_ref, s_ref, e_ref, t):
    parts, both, _ = g_ref.shape
    modes = both // 2
    count = parts // 2
    for n in range(count):
        here = g_ref[n, pl.ds(t, modes, stride=2), :]
        there = g_ref[count + n, pl.ds(1 - t, modes, stride=2), :]
        s_ref[n] = here + there if t == 0 else there - here
    for j in range(count):
        for i in range(j + 1):
            rows, cols = slice(i * LANES, (i + 1) * LANES), slice(j * LANES, (j + 1) * LANES)
            mirror = s_ref[i, cols].T
            value = s_ref[j, rows] - mirror if t == 0 else s_ref[j, rows] + mirror
            at = t * modes + j * LANES
            e_ref[rows, at : at + LANES] = value.astype(BF16)


def prepare_slots(slot_ref, core, flat_ref, pick_ref, mask_ref, part_ref, place_ref):
    count = slot_ref.shape[0]
    chips, rows, modes = pick_ref.shape[0], pick_ref.shape[1] // TM, pick_ref.shape[2]
    tiles = modes // TM
    slots = count // (2 * chips)
    slot = slot_ref[...].reshape(1, count)

    def start(i):
        return i * tiles - (i * (i - 1)) // 2

    edge = 2 * tiles + 1
    root = jnp.sqrt((edge * edge - 8 * slot).astype(F32))
    i = jnp.floor((edge - root) * 0.5).astype(jnp.int32)
    i = jnp.where(start(i) > slot, i - 1, jnp.where(start(i + 1) <= slot, i + 1, i))
    j = slot - start(i) + i
    flat_ref[...] = jnp.full(flat_ref.shape, -1.0, F32)
    flat_ref[0:1, :count] = i.astype(F32)
    flat_ref[1:2, :count] = j.astype(F32)
    column = flat_ref[...].T
    mode = lax.broadcasted_iota(jnp.int32, (rows, modes), 1)
    lane = lax.broadcasted_iota(jnp.int32, (rows, LANES), 1)
    for chip in range(chips):
        at = 2 * chip * slots
        parts = []
        for g in range(GROUPS):
            lo = at + g * (-(-slots // GROUPS))
            part = jnp.where(
                core == 0,
                column[lo : lo + rows // GROUPS, :2],
                column[lo + slots : lo + slots + rows // GROUPS, :2],
            )
            parts.append(part)
        both = jnp.concatenate(parts, 0).astype(jnp.int32)
        i_of, j_of = both[:, :1] * TM, both[:, 1:]
        for r in range(TM):
            pick = jnp.where(mode == i_of + r, 1.0, 0.0)
            pick_ref[chip, r * rows : (r + 1) * rows] = pick.astype(BF16)
        block = j_of // (LANES // TM)
        inside = j_of - block * (LANES // TM)
        part_ref[chip] = jnp.broadcast_to(block, (rows, LANES))
        mask_ref[chip] = jnp.where(lane // TM == inside, 1.0, 0.0)
    row = lax.broadcasted_iota(jnp.int32, (2 * TM * LANES, LANES), 0)
    col = lax.broadcasted_iota(jnp.int32, (2 * TM * LANES, LANES), 1)
    r, t = row // (2 * LANES), (row // LANES) % 2
    target = (t * TM + r) * TM + row % TM
    width = 2 * TM * TM
    for n in range(place_ref.shape[0]):
        place_ref[n] = jnp.where(target + n * width == col, 1.0, 0.0).astype(BF16)


def main_kernel(
    scale,
    seed_ref,
    slot_ref,
    raw_ref,
    out_ref,
    own_ref,
    near_ref,
    y_ref,
    z_ref,
    u_ref,
    f_ref,
    h_ref,
    g_ref,
    s_ref,
    swap_ref,
    got_ref,
    sum_ref,
    flat_ref,
    pick_ref,
    mask_ref,
    part_ref,
    place_ref,
    acc_ref,
    send_ref,
    came_ref,
    send_yz_ref,
    came_yz_ref,
    slots_here,
    seeds_here,
    local_sems,
    small_sems,
    plane_sems,
    tail_sems,
    swap_sems,
    piece_sems,
):
    cfg = lax.axis_index("cfg")
    me = lax.axis_index("sx")
    size = lax.axis_size("sx")
    chips = size // 2
    core = lax.rem(me, 2)
    chip = me // 2
    partner = (cfg, chip * 2 + 1 - core)
    below = (cfg, lax.rem(me + size - 1, size))
    modes, _, blocks, _, _ = raw_ref.shape
    rows = mask_ref.shape[1]
    slots = out_ref.shape[0]

    barrier = pltpu.get_barrier_semaphore()
    for step in range(1, size):
        pl.semaphore_signal(
            barrier,
            inc=1,
            device_id=(cfg, lax.rem(me + step, size)),
            device_id_type=MESH,
        )
    seed_copy = pltpu.make_async_copy(seed_ref, seeds_here, small_sems.at[0])
    seed_copy.start()
    local = []
    for k in range(blocks):
        for c in range(COLOURS):
            local.append(
                pltpu.make_async_copy(
                    raw_ref.at[:, c, k], own_ref.at[k, c], local_sems.at[k, c]
                )
            )
            local[-1].start()
    slot_copy = pltpu.make_async_copy(slot_ref, slots_here, small_sems.at[1])
    slot_copy.start()
    first = me * (blocks * LANES)
    position = lax.broadcasted_iota(
        jnp.int32, (blocks, LANES), 0
    ) * LANES + lax.broadcasted_iota(jnp.int32, (blocks, LANES), 1)
    seed_copy.wait()
    for d in (1, 2, 0):
        code = first + behind(position, d, blocks * LANES)
        for e, value in enumerate(links(seeds_here[d], code)):
            u_ref[d, e] = value
    pl.semaphore_wait(barrier, size - 1)

    def tail(n):
        k, part = blocks - 1, pl.ds(n * LANES, LANES)
        return pltpu.make_async_remote_copy(
            src_ref=own_ref.at[k, :, part],
            dst_ref=near_ref.at[k, :, part],
            send_sem=tail_sems.at[0, n],
            recv_sem=tail_sems.at[1, n],
            device_id=below,
            device_id_type=MESH,
        )

    def plane(k):
        return pltpu.make_async_remote_copy(
            src_ref=own_ref.at[k],
            dst_ref=near_ref.at[k],
            send_sem=plane_sems.at[0, k],
            recv_sem=plane_sems.at[1, k],
            device_id=below,
            device_id_type=MESH,
        )

    for k in range(blocks):
        for c in range(COLOURS):
            local[k * COLOURS + c].wait()
        if k < blocks - 1:
            plane(k).start()
    for n in range(modes // LANES):
        tail(n).start()

    v = own_ref.reshape(blocks, COLOURS, 2 * modes, LANES)
    near = near_ref.reshape(blocks, COLOURS, 2 * modes, LANES)
    shift_modes(v, y_ref, z_ref)
    swap_ref[...] = jnp.zeros_like(swap_ref)
    g_ref[...] = jnp.zeros_like(g_ref)

    def swap(d, t):
        lanes = pl.ds(t * modes, modes)
        return pltpu.make_async_remote_copy(
            src_ref=swap_ref.at[d, :, lanes],
            dst_ref=got_ref.at[d, :, lanes],
            send_sem=swap_sems.at[t, d],
            recv_sem=swap_sems.at[2 + t, d],
            device_id=partner,
            device_id_type=MESH,
        )

    def finish(d, products_ref):
        for t in range(2):
            derive(products_ref, s_ref, swap_ref.at[d], t)
            swap(d, t).start()

    def join(d):
        for t in range(2):
            lanes = slice(t * modes, (t + 1) * modes)
            swap(d, t).wait_recv()
            total = swap_ref[d, :, lanes].astype(F32) + got_ref[d, :, lanes].astype(F32)
            sum_ref[d, :, lanes] = total.astype(BF16)

    def pick(d, to):
        part, mask = part_ref[to], mask_ref[to]
        lines = jnp.dot(pick_ref[to], sum_ref[d], preferred_element_type=F32)
        found = []
        for r in range(TM):
            line = lines[r * rows : (r + 1) * rows]
            for t in range(2):
                at = t * modes
                x = line[:, at : at + LANES]
                for n in range(1, modes // LANES):
                    y = line[:, at + n * LANES : at + (n + 1) * LANES]
                    x = jnp.where(part == n, y, x)
                found.append((x * mask).astype(BF16))
        return jnp.concatenate(found, 1)

    def gather(ds, to):
        found = jnp.concatenate([pick(d, to) for d in ds], 1)
        place = jnp.concatenate([place_ref[m] for m in range(len(ds))], 0)
        lines = jnp.dot(found, place, preferred_element_type=F32)
        sets = GROUPS // len(ds)
        each = rows // sets
        total = lines[:each]
        for n in range(1, sets):
            line = lines[n * each : (n + 1) * each]
            total = total + pltpu.roll(line, n * (LANES // sets), 1)
        return total

    def target(n):
        upper = (2 * chip) // chips
        rising = n + (n - chip + chips) // chips
        falling = chips - 1 - n
        falling = falling - (chip - falling + chips) // chips
        return upper * rising + (1 - upper) * falling

    def piece(kind, to, origin):
        send, came = ((send_ref, came_ref), (send_yz_ref, came_yz_ref))[kind]
        return pltpu.make_async_remote_copy(
            src_ref=send.at[to],
            dst_ref=came.at[origin],
            send_sem=piece_sems.at[2 * kind, to],
            recv_sem=piece_sems.at[2 * kind + 1, origin],
            device_id=(cfg, to * 2 + core),
            device_id_type=MESH,
        )

    def post(kind, ds):
        send = (send_ref, send_yz_ref)[kind]

        def post_step(n, carry):
            to = target(n)
            send[to] = gather(ds, to).astype(BF16)
            if kind == 0:
                piece(kind, to, chip).start()
            return carry

        lax.fori_loop(0, chips - 1, post_step, 0)
        return gather(ds, chip)

    def collect(kind, total):
        came = (came_ref, came_yz_ref)[kind]
        for step in range(1, chips):
            origin = lax.rem(chip + step, chips)
            piece(kind, origin, origin).wait_recv()
            total = total + came[origin].astype(F32)
        return total * scale

    def sent(kind):
        for step in range(1, chips):
            piece(kind, lax.rem(chip + step, chips), chip).wait_send()

    def pair_step(k, carry):
        sites = (2 * k, 2 * k + 1)
        for slot, site in enumerate(sites):
            widen(v, site, f_ref)
            fill_hops(u_ref, 1, f_ref, site, h_ref, slot)
            fill_hops(u_ref, 2, f_ref, site, h_ref, 2 + slot)
        add_products(y_ref, sites, h_ref.at[:2], g_ref.at[0])
        add_products(z_ref, sites, h_ref.at[2:], g_ref.at[1])
        return carry

    lax.fori_loop(0, blocks // 2, pair_step, 0)
    for d in (1, 2):
        finish(d, g_ref.at[d - 1])
    slot_copy.wait()
    prepare_slots(
        slots_here, core, flat_ref, pick_ref, mask_ref, part_ref, place_ref
    )
    for d in (1, 2):
        join(d)

    acc_ref[...] = post(1, (1, 2))
    g_ref[0] = jnp.zeros(g_ref.shape[1:], F32)

    def near_step(k, carry):
        sites = (2 * k, 2 * k + 1)
        for slot, site in enumerate(sites):
            plane(site).wait_recv()
            widen(near, site, f_ref)
            fill_hops(u_ref, 0, f_ref, site, h_ref, slot)
        add_products(v, sites, h_ref, g_ref.at[0])
        return carry

    lax.fori_loop(0, blocks // 2 - 1, near_step, 0)

    def use_part(n):
        lo, hi = n * LANES, (n + 1) * LANES
        widen(near, blocks - 1, f_ref, lo, hi)
        fill_hops(u_ref, 0, f_ref, blocks - 1, h_ref, 0, lo, hi)
        add_block(v, blocks - 1, h_ref, g_ref.at[0], n)

    def use_plane(k):
        widen(near, k, f_ref)
        fill_hops(u_ref, 0, f_ref, k, h_ref, 0)
        add_products(v, (k,), h_ref, g_ref.at[0])

    plane(blocks - 2).wait_recv()
    use_plane(blocks - 2)
    def launch():
        def launch_step(n, carry):
            piece(1, target(n), chip).start()
            return carry

        lax.fori_loop(0, chips - 1, launch_step, 0)

    for n in range(modes // LANES):
        tail(n).wait_recv()
        if n == modes // LANES - 1:
            pl.when(core == 1)(launch)
        use_part(n)
    finish(0, g_ref.at[0])
    for n in range(modes // LANES):
        tail(n).wait_send()
    pl.when(core == 0)(launch)
    join(0)

    here = post(0, (0,))
    per = -(-slots // GROUPS)
    each = rows // GROUPS
    width = 2 * TM * TM

    def place_out(value, sets, columns):
        lanes = LANES // sets
        for g in range(GROUPS):
            take = min(per, slots - g * per)
            n, m = divmod(g, GROUPS // sets)
            part = value[m * each : m * each + take, n * lanes : (n + 1) * lanes]
            out_ref[g * per : g * per + take, columns] = part

    place_out(collect(1, acc_ref[...]), 2, slice(width, 3 * width))
    place_out(collect(0, here), 4, slice(0, width))
    sent(0)
    sent(1)
    for d in range(3):
        for t in range(2):
            swap(d, t).wait_send()
    for k in range(blocks - 1):
        plane(k).wait_send()


def per_device(eigvecs, link_seed, ownership):
    modes, _, colours, layers, sites = eigvecs.shape
    size = lax.axis_size("sx")
    chips = size // 2
    blocks = sites // LANES
    raw = (
        eigvecs.transpose(0, 2, 3, 1, 4)
        .reshape(modes, colours, 2, blocks, LANES)
        .transpose(0, 1, 3, 2, 4)
    )
    count = ownership.shape[0]
    slots = count // size
    per = -(-slots // GROUPS)
    each = -(-per // SUBLANES) * SUBLANES
    rows = GROUPS * each
    flat = -(-(count - slots + (GROUPS - 1) * per + each) // LANES) * LANES
    scale = 1.0 / math.sqrt(12.0 * layers * size * sites)
    vmem = pl.BlockSpec(memory_space=pltpu.VMEM)
    hbm = pl.BlockSpec(memory_space=pltpu.HBM)
    plane = pltpu.VMEM((blocks, colours, modes, 2, LANES), BF16)
    both = 2 * modes
    shifted = pltpu.VMEM((blocks, colours, both, LANES), BF16)
    derived = pltpu.VMEM((3, modes, both), BF16)
    return pl.pallas_call(
        functools.partial(main_kernel, scale),
        out_shape=jax.ShapeDtypeStruct((slots, 6 * TM * TM), F32),
        in_specs=[hbm, hbm, hbm],
        out_specs=vmem,
        scratch_shapes=[
            plane,
            plane,
            shifted,
            shifted,
            pltpu.VMEM((3, 18, blocks, LANES), F32),
            pltpu.VMEM((colours, both, LANES), F32),
            pltpu.VMEM((4, colours, both, LANES), BF16),
            pltpu.VMEM((2, both // LANES, both, LANES), F32),
            pltpu.VMEM((modes // LANES, modes, LANES), F32),
            derived,
            derived,
            derived,
            pltpu.VMEM((8, flat), F32),
            pltpu.VMEM((chips, TM * rows, modes), BF16),
            pltpu.VMEM((chips, rows, LANES), F32),
            pltpu.VMEM((chips, rows, LANES), jnp.int32),
            pltpu.VMEM((2, 2 * TM * LANES, LANES), BF16),
            pltpu.VMEM((2 * each, LANES), F32),
            pltpu.VMEM((chips, each, LANES), BF16),
            pltpu.VMEM((chips, each, LANES), BF16),
            pltpu.VMEM((chips, 2 * each, LANES), BF16),
            pltpu.VMEM((chips, 2 * each, LANES), BF16),
            pltpu.VMEM((count,), jnp.int32),
            pltpu.SMEM(link_seed.shape, jnp.int32),
            pltpu.SemaphoreType.DMA((blocks, colours)),
            pltpu.SemaphoreType.DMA((2,)),
            pltpu.SemaphoreType.DMA((2, blocks)),
            pltpu.SemaphoreType.DMA((2, modes // LANES)),
            pltpu.SemaphoreType.DMA((4, 3)),
            pltpu.SemaphoreType.DMA((4, chips)),
        ],
        compiler_params=pltpu.CompilerParams(
            collective_id=0, has_side_effects=True, vmem_limit_bytes=LARGE
        ),
        name="elementals",
    )(*[pltpu.with_memory_space_constraint(x, pltpu.HBM) for x in (link_seed, ownership, raw)])


def solution(mesh):
    return jax.shard_map(
        per_device,
        mesh=mesh,
        in_specs=(P("cfg", None, None, "sx", None), P("cfg"), P()),
        out_specs=P(("cfg", "sx"), None),
        check_vma=False,
    )
```

```python
import functools
import math

import jax
import jax.numpy as jnp
from jax import lax
from jax.experimental import pallas as pl
from jax.experimental.pallas import tpu as pltpu
from jax.sharding import PartitionSpec as P

TM = 4
NZ = 64
MODULUS = 46337
LANES = 128
ROWS = 16
COLOURS = 3
GROUPS = 4
SUBLANES = 8
LARGE = 52 * 1024 * 1024
MESH = pl.DeviceIdType.MESH
F32 = jnp.float32
BF16 = jnp.bfloat16
NT = (((1,), (1,)), ((), ()))


def quotient(value):
    q = jnp.floor(value.astype(F32) * (1.0 / MODULUS)).astype(jnp.int32)
    rest = value - q * MODULUS
    q = jnp.where(rest < 0, q - 1, jnp.where(rest >= MODULUS, q + 1, q))
    return q


def modulo(value):
    return value - quotient(value) * MODULUS


def links(seed, code):
    high = quotient(code)
    low = code - high * MODULUS
    mixed = modulo(seed * seed + low)
    mixed = modulo(mixed * mixed + high * 977 + 31)
    th = []
    for k in range(7):
        g = modulo(mixed + (5171 * k + 1))
        g = modulo(g * g + low)
        g = modulo(g * g + 12345)
        th.append(g.astype(F32) * (2.0 * math.pi / MODULUS) - math.pi)
    ca, sa = jnp.cos(th[0]), jnp.sin(th[0])
    cb, sb = jnp.cos(th[1]), jnp.sin(th[1])
    cg, sg = jnp.cos(th[2]), jnp.sin(th[2])
    rot = [
        [ca * cb * cg - sa * sg, -ca * cb * sg - sa * cg, ca * sb],
        [sa * cb * cg + ca * sg, -sa * cb * sg + ca * cg, sa * sb],
        [-sb * cg, sb * sg, cb],
    ]
    left = [th[3], th[4], -th[3] - th[4]]
    right = [th[5], th[6], -th[5] - th[6]]
    real, imag = [], []
    for r in range(3):
        for c in range(3):
            angle = left[r] + right[c]
            real.append(rot[r][c] * jnp.cos(angle))
            imag.append(rot[r][c] * jnp.sin(angle))
    return real + imag


def behind(place, d, sites):
    if d == 1:
        return jnp.where(place < NZ, place + (sites - NZ), place - NZ)
    if d == 2:
        return jnp.where(place % NZ == 0, place + (NZ - 1), place - 1)
    return place


def shift_modes(v_ref, y_ref, z_ref):
    blocks = v_ref.shape[0]
    wide = 2 * LANES
    row = lax.broadcasted_iota(jnp.int32, (wide, wide), 0)
    col = lax.broadcasted_iota(jnp.int32, (wide, wide), 1)
    from_y = col + (LANES - NZ)
    from_z = LANES + behind(col - LANES, 2, wide)
    source = jnp.where(col < LANES, from_y, from_z)
    move = (row == source).astype(F32).astype(BF16)

    def step(k, carry):
        before = lax.rem(k + blocks - 1, blocks)
        for c in range(COLOURS):
            both = jnp.concatenate([v_ref[before, c], v_ref[k, c]], 1)
            moved = jnp.dot(both, move, preferred_element_type=F32).astype(BF16)
            y_ref[k, c] = moved[:, :LANES]
            z_ref[k, c] = moved[:, LANES:]
        return carry

    lax.fori_loop(0, blocks, step, 0)


def widen(src_ref, site, f_ref, lo=0, hi=None):
    rows = slice(2 * lo, f_ref.shape[1] if hi is None else 2 * hi)
    for c in range(COLOURS):
        f_ref[c, rows] = src_ref[site, c, rows].astype(F32)


def fill_hops(u_ref, d, f_ref, site, h_ref, slot, lo=0, hi=None):
    modes = f_ref.shape[1] // 2
    hi = modes if hi is None else hi

    def entry(e):
        return jnp.broadcast_to(u_ref[d, e, pl.ds(site, 1), :], (8, LANES))

    u = [entry(e) for e in range(18)]

    def rows_step(g, carry):
        out = [[] for _ in range(6)]
        for lo in (0, 8):
            v = []
            for t in range(2):
                at = pl.multiple_of(2 * g * ROWS, 2 * ROWS) + 2 * lo + t
                for c in range(COLOURS):
                    v.append(f_ref[c, pl.ds(at, 8, stride=2), :])
            for c in range(COLOURS):
                re = im = None
                for k in range(COLOURS):
                    ur, ui = u[3 * c + k], u[9 + 3 * c + k]
                    p = ur * v[k] - ui * v[3 + k]
                    q = ur * v[3 + k] + ui * v[k]
                    re = p if re is None else re + p
                    im = q if im is None else im + q
                out[c].append(re)
                out[3 + c].append(im)
        for q in range(6):
            at = pl.multiple_of((q // 3) * modes + g * ROWS, ROWS)
            both = jnp.concatenate(out[q], 0).astype(BF16)
            h_ref[slot, q % 3, pl.ds(at, ROWS)] = both
        return carry

    lax.fori_loop(lo // ROWS, hi // ROWS, rows_step, 0, unroll=2)


def add_products(w_ref, sites, h_ref, g_ref):
    left = jnp.concatenate(
        [w_ref[site, c] for site in sites for c in range(COLOURS)], 1
    )
    right = jnp.concatenate(
        [h_ref[slot, c] for slot in range(len(sites)) for c in range(COLOURS)], 1
    )
    term = lax.dot_general(left, right, NT, preferred_element_type=F32)
    for n in range(g_ref.shape[0]):
        g_ref[n] += term[:, n * LANES : (n + 1) * LANES]


def add_block(w_ref, site, h_ref, g_ref, n):
    modes = h_ref.shape[2] // 2
    left = jnp.concatenate([w_ref[site, c] for c in range(COLOURS)], 1)
    rows = [slice(t * modes + n * LANES, t * modes + (n + 1) * LANES) for t in range(2)]
    right = jnp.concatenate(
        [
            jnp.concatenate([h_ref[0, c, at] for c in range(COLOURS)], 1)
            for at in rows
        ],
        0,
    )
    term = lax.dot_general(left, right, NT, preferred_element_type=F32)
    g_ref[n] += term[:, :LANES]
    g_ref[modes // LANES + n] += term[:, LANES:]


def derive(g_ref, s_ref, e_ref, t):
    parts, both, _ = g_ref.shape
    modes = both // 2
    count = parts // 2
    for n in range(count):
        here = g_ref[n, pl.ds(t, modes, stride=2), :]
        there = g_ref[count + n, pl.ds(1 - t, modes, stride=2), :]
        s_ref[n] = here + there if t == 0 else there - here
    for j in range(count):
        for i in range(j + 1):
            rows, cols = slice(i * LANES, (i + 1) * LANES), slice(j * LANES, (j + 1) * LANES)
            mirror = s_ref[i, cols].T
            value = s_ref[j, rows] - mirror if t == 0 else s_ref[j, rows] + mirror
            at = t * modes + j * LANES
            e_ref[rows, at : at + LANES] = value.astype(BF16)


def prepare_slots(slot_ref, core, flat_ref, pick_ref, mask_ref, part_ref, place_ref):
    count = slot_ref.shape[0]
    chips, rows, modes = pick_ref.shape[0], pick_ref.shape[1] // TM, pick_ref.shape[2]
    tiles = modes // TM
    slots = count // (2 * chips)
    slot = slot_ref[...].reshape(1, count)

    def start(i):
        return i * tiles - (i * (i - 1)) // 2

    edge = 2 * tiles + 1
    root = jnp.sqrt((edge * edge - 8 * slot).astype(F32))
    i = jnp.floor((edge - root) * 0.5).astype(jnp.int32)
    i = jnp.where(start(i) > slot, i - 1, jnp.where(start(i + 1) <= slot, i + 1, i))
    j = slot - start(i) + i
    flat_ref[...] = jnp.full(flat_ref.shape, -1.0, F32)
    flat_ref[0:1, :count] = i.astype(F32)
    flat_ref[1:2, :count] = j.astype(F32)
    column = flat_ref[...].T
    mode = lax.broadcasted_iota(jnp.int32, (rows, modes), 1)
    lane = lax.broadcasted_iota(jnp.int32, (rows, LANES), 1)
    for chip in range(chips):
        at = 2 * chip * slots
        parts = []
        for g in range(GROUPS):
            lo = at + g * (-(-slots // GROUPS))
            part = jnp.where(
                core == 0,
                column[lo : lo + rows // GROUPS, :2],
                column[lo + slots : lo + slots + rows // GROUPS, :2],
            )
            parts.append(part)
        both = jnp.concatenate(parts, 0).astype(jnp.int32)
        i_of, j_of = both[:, :1] * TM, both[:, 1:]
        for r in range(TM):
            pick = jnp.where(mode == i_of + r, 1.0, 0.0)
            pick_ref[chip, r * rows : (r + 1) * rows] = pick.astype(BF16)
        block = j_of // (LANES // TM)
        inside = j_of - block * (LANES // TM)
        part_ref[chip] = jnp.broadcast_to(block, (rows, LANES))
        mask_ref[chip] = jnp.where(lane // TM == inside, 1.0, 0.0)
    row = lax.broadcasted_iota(jnp.int32, (2 * TM * LANES, LANES), 0)
    col = lax.broadcasted_iota(jnp.int32, (2 * TM * LANES, LANES), 1)
    r, t = row // (2 * LANES), (row // LANES) % 2
    target = (t * TM + r) * TM + row % TM
    width = 2 * TM * TM
    for n in range(place_ref.shape[0]):
        place_ref[n] = jnp.where(target + n * width == col, 1.0, 0.0).astype(BF16)


def main_kernel(
    scale,
    seed_ref,
    slot_ref,
    raw_ref,
    out_ref,
    own_ref,
    near_ref,
    y_ref,
    z_ref,
    u_ref,
    f_ref,
    h_ref,
    g_ref,
    s_ref,
    swap_ref,
    got_ref,
    sum_ref,
    flat_ref,
    pick_ref,
    mask_ref,
    part_ref,
    place_ref,
    acc_ref,
    send_ref,
    came_ref,
    send_yz_ref,
    came_yz_ref,
    slots_here,
    seeds_here,
    local_sems,
    small_sems,
    plane_sems,
    tail_sems,
    swap_sems,
    piece_sems,
):
    cfg = lax.axis_index("cfg")
    me = lax.axis_index("sx")
    size = lax.axis_size("sx")
    chips = size // 2
    core = lax.rem(me, 2)
    chip = me // 2
    partner = (cfg, chip * 2 + 1 - core)
    below = (cfg, lax.rem(me + size - 1, size))
    modes, _, blocks, _, _ = raw_ref.shape
    rows = mask_ref.shape[1]
    slots = out_ref.shape[0]

    barrier = pltpu.get_barrier_semaphore()
    for step in range(1, size):
        pl.semaphore_signal(
            barrier,
            inc=1,
            device_id=(cfg, lax.rem(me + step, size)),
            device_id_type=MESH,
        )
    seed_copy = pltpu.make_async_copy(seed_ref, seeds_here, small_sems.at[0])
    seed_copy.start()
    local = []
    for k in range(blocks):
        for c in range(COLOURS):
            local.append(
                pltpu.make_async_copy(
                    raw_ref.at[:, c, k], own_ref.at[k, c], local_sems.at[k, c]
                )
            )
            local[-1].start()
    slot_copy = pltpu.make_async_copy(slot_ref, slots_here, small_sems.at[1])
    slot_copy.start()
    pl.semaphore_wait(barrier, size - 1)

    def tail(n):
        k, part = blocks - 1, pl.ds(n * LANES, LANES)
        return pltpu.make_async_remote_copy(
            src_ref=own_ref.at[k, :, part],
            dst_ref=near_ref.at[k, :, part],
            send_sem=tail_sems.at[0, n],
            recv_sem=tail_sems.at[1, n],
            device_id=below,
            device_id_type=MESH,
        )

    def plane(k):
        return pltpu.make_async_remote_copy(
            src_ref=own_ref.at[k],
            dst_ref=near_ref.at[k],
            send_sem=plane_sems.at[0, k],
            recv_sem=plane_sems.at[1, k],
            device_id=below,
            device_id_type=MESH,
        )

    for k in range(blocks):
        for c in range(COLOURS):
            local[k * COLOURS + c].wait()
        if k < blocks - 1:
            plane(k).start()
    for n in range(modes // LANES):
        tail(n).start()

    first = me * (blocks * LANES)
    position = lax.broadcasted_iota(
        jnp.int32, (blocks, LANES), 0
    ) * LANES + lax.broadcasted_iota(jnp.int32, (blocks, LANES), 1)
    seed_copy.wait()
    for d in (1, 2, 0):
        code = first + behind(position, d, blocks * LANES)
        for e, value in enumerate(links(seeds_here[d], code)):
            u_ref[d, e] = value

    v = own_ref.reshape(blocks, COLOURS, 2 * modes, LANES)
    near = near_ref.reshape(blocks, COLOURS, 2 * modes, LANES)
    shift_modes(v, y_ref, z_ref)
    swap_ref[...] = jnp.zeros_like(swap_ref)
    g_ref[...] = jnp.zeros_like(g_ref)

    def swap(d, t):
        lanes = pl.ds(t * modes, modes)
        return pltpu.make_async_remote_copy(
            src_ref=swap_ref.at[d, :, lanes],
            dst_ref=got_ref.at[d, :, lanes],
            send_sem=swap_sems.at[t, d],
            recv_sem=swap_sems.at[2 + t, d],
            device_id=partner,
            device_id_type=MESH,
        )

    def finish(d, products_ref):
        for t in range(2):
            derive(products_ref, s_ref, swap_ref.at[d], t)
            swap(d, t).start()

    def join(d):
        for t in range(2):
            lanes = slice(t * modes, (t + 1) * modes)
            swap(d, t).wait_recv()
            total = swap_ref[d, :, lanes].astype(F32) + got_ref[d, :, lanes].astype(F32)
            sum_ref[d, :, lanes] = total.astype(BF16)

    def pick(d, to):
        part, mask = part_ref[to], mask_ref[to]
        lines = jnp.dot(pick_ref[to], sum_ref[d], preferred_element_type=F32)
        found = []
        for r in range(TM):
            line = lines[r * rows : (r + 1) * rows]
            for t in range(2):
                at = t * modes
                x = line[:, at : at + LANES]
                for n in range(1, modes // LANES):
                    y = line[:, at + n * LANES : at + (n + 1) * LANES]
                    x = jnp.where(part == n, y, x)
                found.append((x * mask).astype(BF16))
        return jnp.concatenate(found, 1)

    def gather(ds, to):
        found = jnp.concatenate([pick(d, to) for d in ds], 1)
        place = jnp.concatenate([place_ref[m] for m in range(len(ds))], 0)
        lines = jnp.dot(found, place, preferred_element_type=F32)
        sets = GROUPS // len(ds)
        each = rows // sets
        total = lines[:each]
        for n in range(1, sets):
            line = lines[n * each : (n + 1) * each]
            total = total + pltpu.roll(line, n * (LANES // sets), 1)
        return total

    def target(n):
        upper = (2 * chip) // chips
        rising = n + (n - chip + chips) // chips
        falling = chips - 1 - n
        falling = falling - (chip - falling + chips) // chips
        return upper * rising + (1 - upper) * falling

    def piece(kind, to, origin):
        send, came = ((send_ref, came_ref), (send_yz_ref, came_yz_ref))[kind]
        return pltpu.make_async_remote_copy(
            src_ref=send.at[to],
            dst_ref=came.at[origin],
            send_sem=piece_sems.at[2 * kind, to],
            recv_sem=piece_sems.at[2 * kind + 1, origin],
            device_id=(cfg, to * 2 + core),
            device_id_type=MESH,
        )

    def post(kind, ds):
        send = (send_ref, send_yz_ref)[kind]

        def post_step(n, carry):
            to = target(n)
            send[to] = gather(ds, to).astype(BF16)
            if kind == 0:
                piece(kind, to, chip).start()
            return carry

        lax.fori_loop(0, chips - 1, post_step, 0)
        return gather(ds, chip)

    def collect(kind, total):
        came = (came_ref, came_yz_ref)[kind]
        for step in range(1, chips):
            origin = lax.rem(chip + step, chips)
            piece(kind, origin, origin).wait_recv()
            total = total + came[origin].astype(F32)
        return total * scale

    def sent(kind):
        for step in range(1, chips):
            piece(kind, lax.rem(chip + step, chips), chip).wait_send()

    def pair_step(k, carry):
        sites = (2 * k, 2 * k + 1)
        for slot, site in enumerate(sites):
            widen(v, site, f_ref)
            fill_hops(u_ref, 1, f_ref, site, h_ref, slot)
            fill_hops(u_ref, 2, f_ref, site, h_ref, 2 + slot)
        add_products(y_ref, sites, h_ref.at[:2], g_ref.at[0])
        add_products(z_ref, sites, h_ref.at[2:], g_ref.at[1])
        return carry

    lax.fori_loop(0, blocks // 2, pair_step, 0)
    for d in (1, 2):
        finish(d, g_ref.at[d - 1])
    slot_copy.wait()
    prepare_slots(
        slots_here, core, flat_ref, pick_ref, mask_ref, part_ref, place_ref
    )
    for d in (1, 2):
        join(d)

    acc_ref[...] = post(1, (1, 2))
    g_ref[0] = jnp.zeros(g_ref.shape[1:], F32)

    def near_step(k, carry):
        sites = (2 * k, 2 * k + 1)
        for slot, site in enumerate(sites):
            plane(site).wait_recv()
            widen(near, site, f_ref)
            fill_hops(u_ref, 0, f_ref, site, h_ref, slot)
        add_products(v, sites, h_ref, g_ref.at[0])
        return carry

    lax.fori_loop(0, blocks // 2 - 1, near_step, 0)

    def use_part(n):
        lo, hi = n * LANES, (n + 1) * LANES
        widen(near, blocks - 1, f_ref, lo, hi)
        fill_hops(u_ref, 0, f_ref, blocks - 1, h_ref, 0, lo, hi)
        add_block(v, blocks - 1, h_ref, g_ref.at[0], n)

    def use_plane(k):
        widen(near, k, f_ref)
        fill_hops(u_ref, 0, f_ref, k, h_ref, 0)
        add_products(v, (k,), h_ref, g_ref.at[0])

    plane(blocks - 2).wait_recv()
    use_plane(blocks - 2)
    def launch():
        def launch_step(n, carry):
            piece(1, target(n), chip).start()
            return carry

        lax.fori_loop(0, chips - 1, launch_step, 0)

    for n in range(modes // LANES):
        tail(n).wait_recv()
        use_part(n)
    finish(0, g_ref.at[0])
    for n in range(modes // LANES):
        tail(n).wait_send()
    launch()
    join(0)

    here = post(0, (0,))
    per = -(-slots // GROUPS)
    each = rows // GROUPS
    width = 2 * TM * TM

    def place_out(value, sets, columns):
        lanes = LANES // sets
        for g in range(GROUPS):
            take = min(per, slots - g * per)
            n, m = divmod(g, GROUPS // sets)
            part = value[m * each : m * each + take, n * lanes : (n + 1) * lanes]
            out_ref[g * per : g * per + take, columns] = part

    place_out(collect(1, acc_ref[...]), 2, slice(width, 3 * width))
    place_out(collect(0, here), 4, slice(0, width))
    sent(0)
    sent(1)
    for d in range(3):
        for t in range(2):
            swap(d, t).wait_send()
    for k in range(blocks - 1):
        plane(k).wait_send()


def per_device(eigvecs, link_seed, ownership):
    modes, _, colours, layers, sites = eigvecs.shape
    size = lax.axis_size("sx")
    chips = size // 2
    blocks = sites // LANES
    raw = (
        eigvecs.transpose(0, 2, 3, 1, 4)
        .reshape(modes, colours, 2, blocks, LANES)
        .transpose(0, 1, 3, 2, 4)
    )
    count = ownership.shape[0]
    slots = count // size
    per = -(-slots // GROUPS)
    each = -(-per // SUBLANES) * SUBLANES
    rows = GROUPS * each
    flat = -(-(count - slots + (GROUPS - 1) * per + each) // LANES) * LANES
    scale = 1.0 / math.sqrt(12.0 * layers * size * sites)
    vmem = pl.BlockSpec(memory_space=pltpu.VMEM)
    hbm = pl.BlockSpec(memory_space=pltpu.HBM)
    plane = pltpu.VMEM((blocks, colours, modes, 2, LANES), BF16)
    both = 2 * modes
    shifted = pltpu.VMEM((blocks, colours, both, LANES), BF16)
    derived = pltpu.VMEM((3, modes, both), BF16)
    return pl.pallas_call(
        functools.partial(main_kernel, scale),
        out_shape=jax.ShapeDtypeStruct((slots, 6 * TM * TM), F32),
        in_specs=[hbm, hbm, hbm],
        out_specs=vmem,
        scratch_shapes=[
            plane,
            plane,
            shifted,
            shifted,
            pltpu.VMEM((3, 18, blocks, LANES), F32),
            pltpu.VMEM((colours, both, LANES), F32),
            pltpu.VMEM((4, colours, both, LANES), BF16),
            pltpu.VMEM((2, both // LANES, both, LANES), F32),
            pltpu.VMEM((modes // LANES, modes, LANES), F32),
            derived,
            derived,
            derived,
            pltpu.VMEM((8, flat), F32),
            pltpu.VMEM((chips, TM * rows, modes), BF16),
            pltpu.VMEM((chips, rows, LANES), F32),
            pltpu.VMEM((chips, rows, LANES), jnp.int32),
            pltpu.VMEM((2, 2 * TM * LANES, LANES), BF16),
            pltpu.VMEM((2 * each, LANES), F32),
            pltpu.VMEM((chips, each, LANES), BF16),
            pltpu.VMEM((chips, each, LANES), BF16),
            pltpu.VMEM((chips, 2 * each, LANES), BF16),
            pltpu.VMEM((chips, 2 * each, LANES), BF16),
            pltpu.VMEM((count,), jnp.int32),
            pltpu.SMEM(link_seed.shape, jnp.int32),
            pltpu.SemaphoreType.DMA((blocks, colours)),
            pltpu.SemaphoreType.DMA((2,)),
            pltpu.SemaphoreType.DMA((2, blocks)),
            pltpu.SemaphoreType.DMA((2, modes // LANES)),
            pltpu.SemaphoreType.DMA((4, 3)),
            pltpu.SemaphoreType.DMA((4, chips)),
        ],
        compiler_params=pltpu.CompilerParams(
            collective_id=0, has_side_effects=True, vmem_limit_bytes=LARGE
        ),
        name="elementals",
    )(*[pltpu.with_memory_space_constraint(x, pltpu.HBM) for x in (link_seed, ownership, raw)])


def solution(mesh):
    return jax.shard_map(
        per_device,
        mesh=mesh,
        in_specs=(P("cfg", None, None, "sx", None), P("cfg"), P()),
        out_specs=P(("cfg", "sx"), None),
        check_vma=False,
    )
```

```python
import functools
import math

import jax
import jax.numpy as jnp
from jax import lax
from jax.experimental import pallas as pl
from jax.experimental.pallas import tpu as pltpu
from jax.sharding import PartitionSpec as P

TM = 4
NZ = 64
MODULUS = 46337
LANES = 128
ROWS = 16
COLOURS = 3
GROUPS = 4
SUBLANES = 8
LARGE = 52 * 1024 * 1024
MESH = pl.DeviceIdType.MESH
F32 = jnp.float32
BF16 = jnp.bfloat16
NT = (((1,), (1,)), ((), ()))


def quotient(value):
    q = jnp.floor(value.astype(F32) * (1.0 / MODULUS)).astype(jnp.int32)
    rest = value - q * MODULUS
    q = jnp.where(rest < 0, q - 1, jnp.where(rest >= MODULUS, q + 1, q))
    return q


def modulo(value):
    return value - quotient(value) * MODULUS


def links(seed, code):
    high = quotient(code)
    low = code - high * MODULUS
    mixed = modulo(seed * seed + low)
    mixed = modulo(mixed * mixed + high * 977 + 31)
    th = []
    for k in range(7):
        g = modulo(mixed + (5171 * k + 1))
        g = modulo(g * g + low)
        g = modulo(g * g + 12345)
        th.append(g.astype(F32) * (2.0 * math.pi / MODULUS) - math.pi)
    ca, sa = jnp.cos(th[0]), jnp.sin(th[0])
    cb, sb = jnp.cos(th[1]), jnp.sin(th[1])
    cg, sg = jnp.cos(th[2]), jnp.sin(th[2])
    rot = [
        [ca * cb * cg - sa * sg, -ca * cb * sg - sa * cg, ca * sb],
        [sa * cb * cg + ca * sg, -sa * cb * sg + ca * cg, sa * sb],
        [-sb * cg, sb * sg, cb],
    ]
    left = [th[3], th[4], -th[3] - th[4]]
    right = [th[5], th[6], -th[5] - th[6]]
    real, imag = [], []
    for r in range(3):
        for c in range(3):
            angle = left[r] + right[c]
            real.append(rot[r][c] * jnp.cos(angle))
            imag.append(rot[r][c] * jnp.sin(angle))
    return real + imag


def behind(place, d, sites):
    if d == 1:
        return jnp.where(place < NZ, place + (sites - NZ), place - NZ)
    if d == 2:
        return jnp.where(place % NZ == 0, place + (NZ - 1), place - 1)
    return place


def shift_modes(v_ref, y_ref, z_ref):
    blocks = v_ref.shape[0]
    wide = 2 * LANES
    row = lax.broadcasted_iota(jnp.int32, (wide, wide), 0)
    col = lax.broadcasted_iota(jnp.int32, (wide, wide), 1)
    from_y = col + (LANES - NZ)
    from_z = LANES + behind(col - LANES, 2, wide)
    source = jnp.where(col < LANES, from_y, from_z)
    move = (row == source).astype(F32).astype(BF16)

    def step(k, carry):
        before = lax.rem(k + blocks - 1, blocks)
        for c in range(COLOURS):
            both = jnp.concatenate([v_ref[before, c], v_ref[k, c]], 1)
            moved = jnp.dot(both, move, preferred_element_type=F32).astype(BF16)
            y_ref[k, c] = moved[:, :LANES]
            z_ref[k, c] = moved[:, LANES:]
        return carry

    lax.fori_loop(0, blocks, step, 0)


def widen(src_ref, site, f_ref, lo=0, hi=None):
    rows = slice(2 * lo, f_ref.shape[1] if hi is None else 2 * hi)
    for c in range(COLOURS):
        f_ref[c, rows] = src_ref[site, c, rows].astype(F32)


def fill_hops(u_ref, d, f_ref, site, h_ref, slot, lo=0, hi=None):
    modes = f_ref.shape[1] // 2
    hi = modes if hi is None else hi

    def entry(e):
        return jnp.broadcast_to(u_ref[d, e, pl.ds(site, 1), :], (8, LANES))

    u = [entry(e) for e in range(18)]

    def rows_step(g, carry):
        out = [[] for _ in range(6)]
        for lo in (0, 8):
            v = []
            for t in range(2):
                at = pl.multiple_of(2 * g * ROWS, 2 * ROWS) + 2 * lo + t
                for c in range(COLOURS):
                    v.append(f_ref[c, pl.ds(at, 8, stride=2), :])
            for c in range(COLOURS):
                re = im = None
                for k in range(COLOURS):
                    ur, ui = u[3 * c + k], u[9 + 3 * c + k]
                    p = ur * v[k] - ui * v[3 + k]
                    q = ur * v[3 + k] + ui * v[k]
                    re = p if re is None else re + p
                    im = q if im is None else im + q
                out[c].append(re)
                out[3 + c].append(im)
        for q in range(6):
            at = pl.multiple_of((q // 3) * modes + g * ROWS, ROWS)
            both = jnp.concatenate(out[q], 0).astype(BF16)
            h_ref[slot, q % 3, pl.ds(at, ROWS)] = both
        return carry

    lax.fori_loop(lo // ROWS, hi // ROWS, rows_step, 0, unroll=4)


def add_products(w_ref, sites, h_ref, g_ref):
    left = jnp.concatenate(
        [w_ref[site, c] for site in sites for c in range(COLOURS)], 1
    )
    right = jnp.concatenate(
        [h_ref[slot, c] for slot in range(len(sites)) for c in range(COLOURS)], 1
    )
    term = lax.dot_general(left, right, NT, preferred_element_type=F32)
    for n in range(g_ref.shape[0]):
        g_ref[n] += term[:, n * LANES : (n + 1) * LANES]


def add_block(w_ref, site, h_ref, g_ref, n):
    modes = h_ref.shape[2] // 2
    left = jnp.concatenate([w_ref[site, c] for c in range(COLOURS)], 1)
    rows = [slice(t * modes + n * LANES, t * modes + (n + 1) * LANES) for t in range(2)]
    right = jnp.concatenate(
        [
            jnp.concatenate([h_ref[0, c, at] for c in range(COLOURS)], 1)
            for at in rows
        ],
        0,
    )
    term = lax.dot_general(left, right, NT, preferred_element_type=F32)
    g_ref[n] += term[:, :LANES]
    g_ref[modes // LANES + n] += term[:, LANES:]


def derive(g_ref, s_ref, e_ref, t):
    parts, both, _ = g_ref.shape
    modes = both // 2
    count = parts // 2
    for n in range(count):
        here = g_ref[n, pl.ds(t, modes, stride=2), :]
        there = g_ref[count + n, pl.ds(1 - t, modes, stride=2), :]
        s_ref[n] = here + there if t == 0 else there - here
    for j in range(count):
        for i in range(j + 1):
            rows, cols = slice(i * LANES, (i + 1) * LANES), slice(j * LANES, (j + 1) * LANES)
            mirror = s_ref[i, cols].T
            value = s_ref[j, rows] - mirror if t == 0 else s_ref[j, rows] + mirror
            at = t * modes + j * LANES
            e_ref[rows, at : at + LANES] = value.astype(BF16)


def prepare_slots(slot_ref, core, flat_ref, pick_ref, mask_ref, part_ref, place_ref):
    count = slot_ref.shape[0]
    chips, rows, modes = pick_ref.shape[0], pick_ref.shape[1] // TM, pick_ref.shape[2]
    tiles = modes // TM
    slots = count // (2 * chips)
    slot = slot_ref[...].reshape(1, count)

    def start(i):
        return i * tiles - (i * (i - 1)) // 2

    edge = 2 * tiles + 1
    root = jnp.sqrt((edge * edge - 8 * slot).astype(F32))
    i = jnp.floor((edge - root) * 0.5).astype(jnp.int32)
    i = jnp.where(start(i) > slot, i - 1, jnp.where(start(i + 1) <= slot, i + 1, i))
    j = slot - start(i) + i
    flat_ref[...] = jnp.full(flat_ref.shape, -1.0, F32)
    flat_ref[0:1, :count] = i.astype(F32)
    flat_ref[1:2, :count] = j.astype(F32)
    column = flat_ref[...].T
    mode = lax.broadcasted_iota(jnp.int32, (rows, modes), 1)
    lane = lax.broadcasted_iota(jnp.int32, (rows, LANES), 1)
    for chip in range(chips):
        at = 2 * chip * slots
        parts = []
        for g in range(GROUPS):
            lo = at + g * (-(-slots // GROUPS))
            part = jnp.where(
                core == 0,
                column[lo : lo + rows // GROUPS, :2],
                column[lo + slots : lo + slots + rows // GROUPS, :2],
            )
            parts.append(part)
        both = jnp.concatenate(parts, 0).astype(jnp.int32)
        i_of, j_of = both[:, :1] * TM, both[:, 1:]
        for r in range(TM):
            pick = jnp.where(mode == i_of + r, 1.0, 0.0)
            pick_ref[chip, r * rows : (r + 1) * rows] = pick.astype(BF16)
        block = j_of // (LANES // TM)
        inside = j_of - block * (LANES // TM)
        part_ref[chip] = jnp.broadcast_to(block, (rows, LANES))
        mask_ref[chip] = jnp.where(lane // TM == inside, 1.0, 0.0)
    row = lax.broadcasted_iota(jnp.int32, (2 * TM * LANES, LANES), 0)
    col = lax.broadcasted_iota(jnp.int32, (2 * TM * LANES, LANES), 1)
    r, t = row // (2 * LANES), (row // LANES) % 2
    target = (t * TM + r) * TM + row % TM
    width = 2 * TM * TM
    for n in range(place_ref.shape[0]):
        place_ref[n] = jnp.where(target + n * width == col, 1.0, 0.0).astype(BF16)


def main_kernel(
    scale,
    seed_ref,
    slot_ref,
    raw_ref,
    out_ref,
    own_ref,
    near_ref,
    y_ref,
    z_ref,
    u_ref,
    f_ref,
    h_ref,
    g_ref,
    s_ref,
    swap_ref,
    got_ref,
    sum_ref,
    flat_ref,
    pick_ref,
    mask_ref,
    part_ref,
    place_ref,
    acc_ref,
    send_ref,
    came_ref,
    send_yz_ref,
    came_yz_ref,
    slots_here,
    seeds_here,
    local_sems,
    small_sems,
    plane_sems,
    tail_sems,
    swap_sems,
    piece_sems,
):
    cfg = lax.axis_index("cfg")
    me = lax.axis_index("sx")
    size = lax.axis_size("sx")
    chips = size // 2
    core = lax.rem(me, 2)
    chip = me // 2
    partner = (cfg, chip * 2 + 1 - core)
    below = (cfg, lax.rem(me + size - 1, size))
    modes, _, blocks, _, _ = raw_ref.shape
    rows = mask_ref.shape[1]
    slots = out_ref.shape[0]

    barrier = pltpu.get_barrier_semaphore()
    for step in range(1, size):
        pl.semaphore_signal(
            barrier,
            inc=1,
            device_id=(cfg, lax.rem(me + step, size)),
            device_id_type=MESH,
        )
    seed_copy = pltpu.make_async_copy(seed_ref, seeds_here, small_sems.at[0])
    seed_copy.start()
    local = []
    for k in range(blocks):
        for c in range(COLOURS):
            local.append(
                pltpu.make_async_copy(
                    raw_ref.at[:, c, k], own_ref.at[k, c], local_sems.at[k, c]
                )
            )
            local[-1].start()
    slot_copy = pltpu.make_async_copy(slot_ref, slots_here, small_sems.at[1])
    slot_copy.start()
    pl.semaphore_wait(barrier, size - 1)

    def tail(n):
        k, part = blocks - 1, pl.ds(n * LANES, LANES)
        return pltpu.make_async_remote_copy(
            src_ref=own_ref.at[k, :, part],
            dst_ref=near_ref.at[k, :, part],
            send_sem=tail_sems.at[0, n],
            recv_sem=tail_sems.at[1, n],
            device_id=below,
            device_id_type=MESH,
        )

    def plane(k):
        return pltpu.make_async_remote_copy(
            src_ref=own_ref.at[k],
            dst_ref=near_ref.at[k],
            send_sem=plane_sems.at[0, k],
            recv_sem=plane_sems.at[1, k],
            device_id=below,
            device_id_type=MESH,
        )

    for k in range(blocks):
        for c in range(COLOURS):
            local[k * COLOURS + c].wait()
        if k < blocks - 1:
            plane(k).start()
    for n in range(modes // LANES):
        tail(n).start()

    first = me * (blocks * LANES)
    position = lax.broadcasted_iota(
        jnp.int32, (blocks, LANES), 0
    ) * LANES + lax.broadcasted_iota(jnp.int32, (blocks, LANES), 1)
    seed_copy.wait()
    for d in (1, 2, 0):
        code = first + behind(position, d, blocks * LANES)
        for e, value in enumerate(links(seeds_here[d], code)):
            u_ref[d, e] = value

    v = own_ref.reshape(blocks, COLOURS, 2 * modes, LANES)
    near = near_ref.reshape(blocks, COLOURS, 2 * modes, LANES)
    shift_modes(v, y_ref, z_ref)
    swap_ref[...] = jnp.zeros_like(swap_ref)
    g_ref[...] = jnp.zeros_like(g_ref)

    def swap(d, t):
        lanes = pl.ds(t * modes, modes)
        return pltpu.make_async_remote_copy(
            src_ref=swap_ref.at[d, :, lanes],
            dst_ref=got_ref.at[d, :, lanes],
            send_sem=swap_sems.at[t, d],
            recv_sem=swap_sems.at[2 + t, d],
            device_id=partner,
            device_id_type=MESH,
        )

    def finish(d, products_ref):
        for t in range(2):
            derive(products_ref, s_ref, swap_ref.at[d], t)
            swap(d, t).start()

    def join(d):
        for t in range(2):
            lanes = slice(t * modes, (t + 1) * modes)
            swap(d, t).wait_recv()
            total = swap_ref[d, :, lanes].astype(F32) + got_ref[d, :, lanes].astype(F32)
            sum_ref[d, :, lanes] = total.astype(BF16)

    def pick(d, to):
        part, mask = part_ref[to], mask_ref[to]
        lines = jnp.dot(pick_ref[to], sum_ref[d], preferred_element_type=F32)
        found = []
        for r in range(TM):
            line = lines[r * rows : (r + 1) * rows]
            for t in range(2):
                at = t * modes
                x = line[:, at : at + LANES]
                for n in range(1, modes // LANES):
                    y = line[:, at + n * LANES : at + (n + 1) * LANES]
                    x = jnp.where(part == n, y, x)
                found.append((x * mask).astype(BF16))
        return jnp.concatenate(found, 1)

    def gather(ds, to):
        found = jnp.concatenate([pick(d, to) for d in ds], 1)
        place = jnp.concatenate([place_ref[m] for m in range(len(ds))], 0)
        lines = jnp.dot(found, place, preferred_element_type=F32)
        sets = GROUPS // len(ds)
        each = rows // sets
        total = lines[:each]
        for n in range(1, sets):
            line = lines[n * each : (n + 1) * each]
            total = total + pltpu.roll(line, n * (LANES // sets), 1)
        return total

    def target(n):
        upper = (2 * chip) // chips
        rising = n + (n - chip + chips) // chips
        falling = chips - 1 - n
        falling = falling - (chip - falling + chips) // chips
        return upper * rising + (1 - upper) * falling

    def piece(kind, to, origin):
        send, came = ((send_ref, came_ref), (send_yz_ref, came_yz_ref))[kind]
        return pltpu.make_async_remote_copy(
            src_ref=send.at[to],
            dst_ref=came.at[origin],
            send_sem=piece_sems.at[2 * kind, to],
            recv_sem=piece_sems.at[2 * kind + 1, origin],
            device_id=(cfg, to * 2 + core),
            device_id_type=MESH,
        )

    def post(kind, ds):
        send = (send_ref, send_yz_ref)[kind]

        def post_step(n, carry):
            to = target(n)
            send[to] = gather(ds, to).astype(BF16)
            if kind == 0:
                piece(kind, to, chip).start()
            return carry

        lax.fori_loop(0, chips - 1, post_step, 0)
        return gather(ds, chip)

    def collect(kind, total):
        came = (came_ref, came_yz_ref)[kind]
        for step in range(1, chips):
            origin = lax.rem(chip + step, chips)
            piece(kind, origin, origin).wait_recv()
            total = total + came[origin].astype(F32)
        return total * scale

    def sent(kind):
        for step in range(1, chips):
            piece(kind, lax.rem(chip + step, chips), chip).wait_send()

    def pair_step(k, carry):
        sites = (2 * k, 2 * k + 1)
        for slot, site in enumerate(sites):
            widen(v, site, f_ref)
            fill_hops(u_ref, 1, f_ref, site, h_ref, slot)
            fill_hops(u_ref, 2, f_ref, site, h_ref, 2 + slot)
        add_products(y_ref, sites, h_ref.at[:2], g_ref.at[0])
        add_products(z_ref, sites, h_ref.at[2:], g_ref.at[1])
        return carry

    lax.fori_loop(0, blocks // 2, pair_step, 0)
    for d in (1, 2):
        finish(d, g_ref.at[d - 1])
    slot_copy.wait()
    prepare_slots(
        slots_here, core, flat_ref, pick_ref, mask_ref, part_ref, place_ref
    )
    for d in (1, 2):
        join(d)

    acc_ref[...] = post(1, (1, 2))
    g_ref[0] = jnp.zeros(g_ref.shape[1:], F32)

    def near_step(k, carry):
        sites = (2 * k, 2 * k + 1)
        for slot, site in enumerate(sites):
            plane(site).wait_recv()
            widen(near, site, f_ref)
            fill_hops(u_ref, 0, f_ref, site, h_ref, slot)
        add_products(v, sites, h_ref, g_ref.at[0])
        return carry

    lax.fori_loop(0, blocks // 2 - 1, near_step, 0)

    def use_part(n):
        lo, hi = n * LANES, (n + 1) * LANES
        widen(near, blocks - 1, f_ref, lo, hi)
        fill_hops(u_ref, 0, f_ref, blocks - 1, h_ref, 0, lo, hi)
        add_block(v, blocks - 1, h_ref, g_ref.at[0], n)

    def use_plane(k):
        widen(near, k, f_ref)
        fill_hops(u_ref, 0, f_ref, k, h_ref, 0)
        add_products(v, (k,), h_ref, g_ref.at[0])

    plane(blocks - 2).wait_recv()
    use_plane(blocks - 2)
    def launch():
        def launch_step(n, carry):
            piece(1, target(n), chip).start()
            return carry

        lax.fori_loop(0, chips - 1, launch_step, 0)

    for n in range(modes // LANES):
        tail(n).wait_recv()
        use_part(n)
    finish(0, g_ref.at[0])
    for n in range(modes // LANES):
        tail(n).wait_send()
    launch()
    join(0)

    here = post(0, (0,))
    per = -(-slots // GROUPS)
    each = rows // GROUPS
    width = 2 * TM * TM

    def place_out(value, sets, columns):
        lanes = LANES // sets
        for g in range(GROUPS):
            take = min(per, slots - g * per)
            n, m = divmod(g, GROUPS // sets)
            part = value[m * each : m * each + take, n * lanes : (n + 1) * lanes]
            out_ref[g * per : g * per + take, columns] = part

    place_out(collect(1, acc_ref[...]), 2, slice(width, 3 * width))
    place_out(collect(0, here), 4, slice(0, width))
    sent(0)
    sent(1)
    for d in range(3):
        for t in range(2):
            swap(d, t).wait_send()
    for k in range(blocks - 1):
        plane(k).wait_send()


def per_device(eigvecs, link_seed, ownership):
    modes, _, colours, layers, sites = eigvecs.shape
    size = lax.axis_size("sx")
    chips = size // 2
    blocks = sites // LANES
    raw = (
        eigvecs.transpose(0, 2, 3, 1, 4)
        .reshape(modes, colours, 2, blocks, LANES)
        .transpose(0, 1, 3, 2, 4)
    )
    count = ownership.shape[0]
    slots = count // size
    per = -(-slots // GROUPS)
    each = -(-per // SUBLANES) * SUBLANES
    rows = GROUPS * each
    flat = -(-(count - slots + (GROUPS - 1) * per + each) // LANES) * LANES
    scale = 1.0 / math.sqrt(12.0 * layers * size * sites)
    vmem = pl.BlockSpec(memory_space=pltpu.VMEM)
    hbm = pl.BlockSpec(memory_space=pltpu.HBM)
    plane = pltpu.VMEM((blocks, colours, modes, 2, LANES), BF16)
    both = 2 * modes
    shifted = pltpu.VMEM((blocks, colours, both, LANES), BF16)
    derived = pltpu.VMEM((3, modes, both), BF16)
    return pl.pallas_call(
        functools.partial(main_kernel, scale),
        out_shape=jax.ShapeDtypeStruct((slots, 6 * TM * TM), F32),
        in_specs=[hbm, hbm, hbm],
        out_specs=vmem,
        scratch_shapes=[
            plane,
            plane,
            shifted,
            shifted,
            pltpu.VMEM((3, 18, blocks, LANES), F32),
            pltpu.VMEM((colours, both, LANES), F32),
            pltpu.VMEM((4, colours, both, LANES), BF16),
            pltpu.VMEM((2, both // LANES, both, LANES), F32),
            pltpu.VMEM((modes // LANES, modes, LANES), F32),
            derived,
            derived,
            derived,
            pltpu.VMEM((8, flat), F32),
            pltpu.VMEM((chips, TM * rows, modes), BF16),
            pltpu.VMEM((chips, rows, LANES), F32),
            pltpu.VMEM((chips, rows, LANES), jnp.int32),
            pltpu.VMEM((2, 2 * TM * LANES, LANES), BF16),
            pltpu.VMEM((2 * each, LANES), F32),
            pltpu.VMEM((chips, each, LANES), BF16),
            pltpu.VMEM((chips, each, LANES), BF16),
            pltpu.VMEM((chips, 2 * each, LANES), BF16),
            pltpu.VMEM((chips, 2 * each, LANES), BF16),
            pltpu.VMEM((count,), jnp.int32),
            pltpu.SMEM(link_seed.shape, jnp.int32),
            pltpu.SemaphoreType.DMA((blocks, colours)),
            pltpu.SemaphoreType.DMA((2,)),
            pltpu.SemaphoreType.DMA((2, blocks)),
            pltpu.SemaphoreType.DMA((2, modes // LANES)),
            pltpu.SemaphoreType.DMA((4, 3)),
            pltpu.SemaphoreType.DMA((4, chips)),
        ],
        compiler_params=pltpu.CompilerParams(
            collective_id=0, has_side_effects=True, vmem_limit_bytes=LARGE
        ),
        name="elementals",
    )(*[pltpu.with_memory_space_constraint(x, pltpu.HBM) for x in (link_seed, ownership, raw)])


def solution(mesh):
    return jax.shard_map(
        per_device,
        mesh=mesh,
        in_specs=(P("cfg", None, None, "sx", None), P("cfg"), P()),
        out_specs=P(("cfg", "sx"), None),
        check_vma=False,
    )
```
